32 devices in a mesh: row: 4 (over z), col: 8 (over y, x, core).
Axes of the slice: x: 2, y: 2, z: 4, core: 2. Of those that a mesh axis runs over, the one named last changes fastest.
Arguments:
- front_panel: float32 [20480, 512], P('row', 'col'), may hold values from -16 to 48, as said below
- front_slab: float32 [20480, 8192], P('row', 'col'), may hold values from -6 to 6
- child_one: bfloat16 [4096, 8192], P('col', 'row'), may hold values from -6 to 6
- child_two: bfloat16 [4096, 8192], P('col', 'row'), may hold values from -6 to 6
- map_one: int32 [16], replicated, may hold values from 0 to 79, as said below
- map_two: int32 [16], replicated, may hold values from 0 to 79, as said below
Outputs:
- factor_panel: float32 [20480, 512], P('row', 'col')
- slab_out: float32 [20480, 8192], P('row', 'col')
The draws below stay inside these ranges and needn't reach their ends.
Inputs may be any that keep to these rules, and one draw needn't show every extreme that they name: `front_panel`: its first 512 rows are, in all 512 columns, a symmetric positive definite block. `map_one`: distinct root row blocks. Of the 20 blocks of one index of row (numbers k * 20 to (k + 1) * 20 - 1) at most 8 are named, and exactly 8 for some index of row. `map_two`: as map_one, drawn independently.
All inputs are finite; a program needn't handle non-finite values.
Results may differ from the reference program's by a relative error of at most 0.0003.
Values may be sent and summed in bfloat16 or wider, within the bound.
No kernel may reach another device: no remote copies, remote signals or barrier semaphores. Data moves between devices by JAX's collectives and lax.ppermute only.
A program may use at most 192 MiB of HBM per device.

```python
import jax
import jax.numpy as jnp
from jax import lax

P_SIZE = 256
SLAB = 8192
BLK = 256
M = 20480
CRB = 16
CR = 4096
RB = 20
OWNERS = 4
CAPB = 8
N_ROW = 4
N_COL = 8


def draw_front_panel(key, part):
    width = 2 * P_SIZE
    keys = jax.random.split(key, 2)
    base = jax.random.normal(keys[0], (width, width), jnp.float32)
    below = jnp.clip(jax.random.normal(keys[1], (M - width, width), jnp.float32), -6.0, 6.0)
    gram = jnp.dot(base, base.T, precision=lax.Precision.HIGHEST) / width
    gram = 0.5 * (gram + gram.T)
    top = 8.0 * (gram + jnp.eye(width, dtype=jnp.float32))
    return jnp.concatenate([top, below], 0).astype(jnp.float32)


def routed_blocks(key):
    keys = jax.random.split(key, 4)
    busiest = jax.random.randint(keys[0], (), 0, OWNERS)
    owner_keys = jax.random.split(keys[1], OWNERS)
    picks = jax.vmap(lambda single: jax.random.permutation(single, RB)[:CAPB])(owner_keys)
    owners = jnp.arange(OWNERS, dtype=jnp.int32)[:, None]
    blocks = (owners * RB + picks.astype(jnp.int32)).reshape(-1)
    owner_flat = jnp.broadcast_to(owners, (OWNERS, CAPB)).reshape(-1)
    order = jax.random.permutation(keys[2], OWNERS * CAPB).astype(jnp.int32)
    score = jnp.where(owner_flat == busiest, 0, order + 1)
    chosen = blocks[jnp.argsort(score, stable=True)[:CRB]]
    return chosen[jax.random.permutation(keys[3], CRB)].astype(jnp.int32)


def draw_map_one(key, part):
    return routed_blocks(jax.random.fold_in(key, 11))


def draw_map_two(key, part):
    return routed_blocks(jax.random.fold_in(key, 23))


def levels(rng, extent, pieces, least, top_value):
    loudness = 1.0
    for position, parts in pieces:
        steps = jax.random.uniform(jax.random.fold_in(jax.random.fold_in(rng, 6), position), (parts,), jnp.float32, least / len(pieces), top_value / len(pieces))
        loudness = loudness * jnp.repeat(jnp.exp(steps), extent[position] // parts).reshape((-1,) + (1,) * (len(extent) - 1 - position))
    return loudness


def noise(key, dims, deviation, limit, cuts=(), kind=jnp.bfloat16):
    result = deviation * jax.random.normal(key, dims, jnp.float32)
    if cuts:
        result = result * levels(key, dims, cuts, -0.22, 0.18)
    return jnp.clip(result, -limit, limit).astype(kind)


def setup_inputs(seed: int = 0) -> dict:
    splits = jax.random.split(jax.random.key(seed), 7)
    front_panel = draw_front_panel(jax.random.fold_in(splits[6], 71), 0)
    front_slab = noise(splits[1], (M, SLAB), 1.0, 6.0, ((0, 4), (1, 8)), jnp.float32)
    child_one = noise(splits[2], (CR, SLAB), 1.0, 6.0, ((0, 8), (1, 4)))
    child_two = noise(splits[3], (CR, SLAB), 1.0, 6.0, ((0, 8), (1, 4)))
    map_one = draw_map_one(jax.random.fold_in(splits[6], 71), 0)
    map_two = draw_map_two(jax.random.fold_in(splits[6], 71), 0)
    return dict(front_panel=front_panel, front_slab=front_slab, child_one=child_one, child_two=child_two, map_one=map_one, map_two=map_two)


def extend(slab, child, mapping):
    piece = SLAB // (N_ROW * N_COL)
    moved = child.astype(jnp.float32).reshape(CR, N_ROW, N_COL, piece)
    moved = jnp.transpose(moved, (0, 2, 1, 3)).reshape(CR, SLAB)
    target = (mapping[:, None] * BLK + jnp.arange(BLK, dtype=jnp.int32)[None, :]).reshape(-1).astype(jnp.int32)
    return slab.at[target].add(moved)

def inverse_factor(block):
    lower = jnp.linalg.cholesky(block)
    identity = jnp.eye(P_SIZE, dtype=jnp.float32)
    return jax.scipy.linalg.solve_triangular(lower, identity, lower=True)

def reference(front_panel, front_slab, child_one, child_two, map_one, map_two):
    highest = lax.Precision.HIGHEST
    assembled = extend(extend(front_slab, child_one, map_one), child_two, map_two)
    inverse_one = inverse_factor(front_panel[:P_SIZE, :P_SIZE])
    first_cols = jnp.dot(front_panel[:, :P_SIZE].astype(jnp.float32), inverse_one.T.astype(jnp.float32), precision=highest, preferred_element_type=jnp.float32)
    second_in = front_panel[:, P_SIZE:] - jnp.dot(first_cols.astype(jnp.float32), first_cols[P_SIZE:2 * P_SIZE].T.astype(jnp.float32), precision=highest, preferred_element_type=jnp.float32)
    inverse_two = inverse_factor(second_in[P_SIZE:2 * P_SIZE])
    second_cols = jnp.dot(second_in.astype(jnp.float32), inverse_two.T.astype(jnp.float32), precision=highest, preferred_element_type=jnp.float32)
    factor_panel = jnp.concatenate([first_cols, second_cols], 1)
    keep = (jnp.arange(M, dtype=jnp.int32) >= 2 * P_SIZE)[:, None]
    masked = jnp.where(keep, factor_panel, jnp.zeros_like(factor_panel))
    slab_rows = factor_panel[2 * P_SIZE:2 * P_SIZE + SLAB]
    slab_out = assembled - jnp.dot(masked.astype(jnp.float32), slab_rows.T.astype(jnp.float32), precision=highest, preferred_element_type=jnp.float32)
    return (factor_panel, slab_out)
```

```python
import functools

import jax
import jax.numpy as jnp
from jax import lax
from jax.experimental import pallas as pl
from jax.experimental.pallas import tpu as pltpu
from jax.sharding import PartitionSpec as P

P_SIZE = 256
BLK = 256
SUB = 32
VMEM_BYTES = 56 * 1024 * 1024


def split_pair(value):
    high = value.astype(jnp.bfloat16)
    low = (value - high.astype(jnp.float32)).astype(jnp.bfloat16)
    return high, low


def dot3(a_high, a_low, b_high, b_low):
    def one(x, y):
        return jnp.dot(x, y, preferred_element_type=jnp.float32)

    return one(a_high, b_high) + (one(a_low, b_high) + one(a_high, b_low))


def exact_dot(a, b, contract):
    return lax.dot_general(
        a,
        b,
        (contract, ((), ())),
        precision=lax.Precision.HIGHEST,
        preferred_element_type=jnp.float32,
    )


def block_inverse(block):
    rows = lax.broadcasted_iota(jnp.int32, (SUB, SUB), 0)
    cols = lax.broadcasted_iota(jnp.int32, (SUB, SUB), 1)
    left = block
    right = (rows == cols).astype(jnp.float32)
    scale = jnp.zeros((SUB, 1), jnp.float32)
    row_of = lax.broadcasted_iota(jnp.int32, (SUB, 1), 0)
    for j in range(SUB):
        pivot = left[j : j + 1, j : j + 1]
        scale = jnp.where(row_of == j, pivot, scale)
        factor = jnp.where(row_of > j, left[:, j : j + 1] / pivot, 0.0)
        if j + 1 < SUB:
            left = left - factor * left[j : j + 1, :]
            right = right - factor * right[j : j + 1, :]
    return right / jnp.sqrt(scale)


def inverse_kernel(top_ref, high_ref, low_ref, work_ref):
    size = top_ref.shape[0]
    work_ref[...] = top_ref[...]
    for start in range(0, size, SUB):
        stop = start + SUB
        inverse = block_inverse(work_ref[start:stop, start:stop])
        lanes = lax.broadcasted_iota(jnp.int32, (SUB, size), 1)
        inside = (lanes >= start) & (lanes < stop)
        rows = exact_dot(inverse, jnp.where(inside, 0.0, work_ref[start:stop, :]), ((1,), (0,)))
        wide = jnp.concatenate([inverse] * (128 // SUB), 1)
        wide = jnp.concatenate([wide] * (size // 128), 1)
        rows = jnp.where(inside, wide, rows)
        if stop < size:
            below = exact_dot(work_ref[stop:size, start:stop], inverse, ((1,), (1,)))
            lanes_b = lax.broadcasted_iota(jnp.int32, (size - stop, size), 1)
            inside_b = (lanes_b >= start) & (lanes_b < stop)
            kept = jnp.where(inside_b, 0.0, work_ref[stop:size, :])
            work_ref[stop:size, :] = kept - exact_dot(below, rows, ((1,), (0,)))
        work_ref[start:stop, :] = jnp.where(lanes < stop, rows, 0.0)
    high, low = split_pair(work_ref[...])
    high_ref[...] = high
    low_ref[...] = low


def factor_inverse(top):
    size = top.shape[0]
    pair = jax.ShapeDtypeStruct((size, size), jnp.bfloat16)
    return pl.pallas_call(
        inverse_kernel,
        out_shape=(pair, pair),
        scratch_shapes=[pltpu.VMEM((size, size), jnp.float32)],
        compiler_params=pltpu.CompilerParams(vmem_limit_bytes=VMEM_BYTES),
        cost_estimate=pl.CostEstimate(flops=size * size * 60000, transcendentals=0, bytes_accessed=2 * size * size * 4),
        name="factor_inverse",
    )(top)


def panel_kernel(rank_ref, high_ref, low_ref, panel_ref, fhigh_ref, flow_ref, own_ref, work_ref):
    p_high, p_low = split_pair(panel_ref[...])
    work_ref[...] = dot3(high_ref[...], low_ref[...], p_high, p_low)
    own = own_ref.shape[0]
    own_ref[...] = work_ref[pl.ds(pl.multiple_of(rank_ref[0] * own, 8), own), :]
    f_high, f_low = split_pair(work_ref[...].T)
    fhigh_ref[...] = f_high
    flow_ref[...] = f_low


def panel_rows(high, low, gathered, rank, own):
    size, rows = gathered.shape
    tile = 512
    pair = jax.ShapeDtypeStruct((rows, size), jnp.bfloat16)
    return pl.pallas_call(
        panel_kernel,
        grid_spec=pltpu.PrefetchScalarGridSpec(
            num_scalar_prefetch=1,
            grid=(rows // tile,),
            in_specs=[
                pl.BlockSpec((size, size), lambda i, r: (0, 0)),
                pl.BlockSpec((size, size), lambda i, r: (0, 0)),
                pl.BlockSpec((size, tile), lambda i, r: (0, i)),
            ],
            out_specs=[
                pl.BlockSpec((tile, size), lambda i, r: (i, 0)),
                pl.BlockSpec((tile, size), lambda i, r: (i, 0)),
                pl.BlockSpec((own, tile), lambda i, r: (0, i)),
            ],
            scratch_shapes=[pltpu.VMEM((size, tile), jnp.float32)],
        ),
        out_shape=(pair, pair, jax.ShapeDtypeStruct((own, rows), jnp.float32)),
        compiler_params=pltpu.CompilerParams(vmem_limit_bytes=VMEM_BYTES),
        cost_estimate=pl.CostEstimate(flops=6 * rows * size * size, transcendentals=0, bytes_accessed=8 * rows * size),
        name="panel_rows",
    )(rank, high, low, gathered)


def slab_rows_kernel(high_ref, low_ref, panel_ref, bhigh_ref, blow_ref):
    p_high, p_low = split_pair(panel_ref[...])
    b_high, b_low = split_pair(dot3(high_ref[...], low_ref[...], p_high, p_low))
    bhigh_ref[...] = b_high
    blow_ref[...] = b_low


def slab_rows(high, low, wanted):
    size, rows = wanted.shape
    tile = 512
    pair = jax.ShapeDtypeStruct((size, rows), jnp.bfloat16)
    whole = pl.BlockSpec((size, size), lambda i: (0, 0))
    part = pl.BlockSpec((size, tile), lambda i: (0, i))
    return pl.pallas_call(
        slab_rows_kernel,
        grid=(rows // tile,),
        in_specs=[whole, whole, part],
        out_specs=[part, part],
        out_shape=(pair, pair),
        compiler_params=pltpu.CompilerParams(vmem_limit_bytes=VMEM_BYTES),
        cost_estimate=pl.CostEstimate(flops=6 * rows * size * size, transcendentals=0, bytes_accessed=8 * rows * size),
        name="slab_rows",
    )(high, low, wanted)


def add_pieces(out_ref, child_ref):
    pieces, piece = child_ref.shape[0], child_ref.shape[3]
    for a in range(pieces):
        cols = slice(a * piece, (a + 1) * piece)
        out_ref[:, cols] = out_ref[:, cols] + child_ref[a, 0].astype(jnp.float32)


def update_kernel(table_ref, fhigh_ref, flow_ref, bhigh_ref, blow_ref, slab_ref, child_ref, out_ref):
    step = pl.program_id(0)

    @pl.when(step < table_ref[2, 0])
    def _():
        out_ref[...] = slab_ref[...]

    @pl.when(step >= table_ref[2, 0])
    def _():
        out_ref[...] = slab_ref[...] - dot3(fhigh_ref[...], flow_ref[...], bhigh_ref[...], blow_ref[...])

    @pl.when(table_ref[1, step] > 0)
    def _():
        add_pieces(out_ref, child_ref)


def update_slab(table, f_high, f_low, b_high, b_low, slab, child):
    rows, width = slab.shape
    size = f_high.shape[1]
    rowspec = pl.BlockSpec((BLK, size), lambda i, t: (i, 0))
    bspec = pl.BlockSpec((size, width), lambda i, t: (0, 0))
    tile = pl.BlockSpec((BLK, width), lambda i, t: (i, 0))
    pieces, piece = child.shape[0], child.shape[3]
    return pl.pallas_call(
        update_kernel,
        grid_spec=pltpu.PrefetchScalarGridSpec(
            num_scalar_prefetch=1,
            grid=(rows // BLK,),
            in_specs=[
                rowspec,
                rowspec,
                bspec,
                bspec,
                tile,
                pl.BlockSpec((pieces, 1, BLK, piece), lambda i, t: (0, t[0, i], 0, 0)),
            ],
            out_specs=tile,
        ),
        out_shape=jax.ShapeDtypeStruct((rows, width), jnp.float32),
        compiler_params=pltpu.CompilerParams(vmem_limit_bytes=VMEM_BYTES),
        cost_estimate=pl.CostEstimate(flops=6 * rows * size * width, transcendentals=0, bytes_accessed=8 * rows * width),
        name="update_slab",
    )(table, f_high, f_low, b_high, b_low, slab, child)


def place_kernel(table_ref, child_ref, slab_ref, out_ref):
    step = pl.program_id(0)
    first = (step == 0) | (table_ref[0, step] != table_ref[0, jnp.maximum(step - 1, 0)])

    @pl.when(first)
    def _():
        out_ref[...] = slab_ref[...]

    @pl.when(table_ref[1, step] > 0)
    def _():
        add_pieces(out_ref, child_ref)


def place_child(table, child, slab):
    rows, width = slab.shape
    pieces, slots, _, piece = child.shape
    tile = pl.BlockSpec((BLK, width), lambda i, t: (t[0, i], 0))
    return pl.pallas_call(
        place_kernel,
        grid_spec=pltpu.PrefetchScalarGridSpec(
            num_scalar_prefetch=1,
            grid=(slots,),
            in_specs=[pl.BlockSpec((pieces, 1, BLK, piece), lambda i, t: (0, t[2, i], 0, 0)), tile],
            out_specs=tile,
        ),
        out_shape=jax.ShapeDtypeStruct((rows, width), jnp.float32),
        input_output_aliases={2: 0},
        compiler_params=pltpu.CompilerParams(vmem_limit_bytes=VMEM_BYTES),
        cost_estimate=pl.CostEstimate(flops=0, transcendentals=0, bytes_accessed=8 * slots * BLK * width),
        name="place_child",
    )(table, child, slab)


def pack_kernel(table_ref, block_ref, out_ref):
    out_ref[...] = block_ref[...]


def pack_blocks(table, blocks):
    slots = table.shape[0]
    _, height, piece = blocks.shape
    return pl.pallas_call(
        pack_kernel,
        grid_spec=pltpu.PrefetchScalarGridSpec(
            num_scalar_prefetch=1,
            grid=(slots,),
            in_specs=[pl.BlockSpec((1, height, piece), lambda i, t: (t[i], 0, 0))],
            out_specs=pl.BlockSpec((1, height, piece), lambda i, t: (i, 0, 0)),
        ),
        out_shape=jax.ShapeDtypeStruct((slots, height, piece), blocks.dtype),
        cost_estimate=pl.CostEstimate(flops=0, transcendentals=0, bytes_accessed=4 * slots * height * piece),
        name="pack_blocks",
    )(table, blocks)


def last_kept(values, kept):
    count = values.shape[0]
    at = jnp.arange(count, dtype=jnp.int32)
    before = (at[None, :] <= at[:, None]) & kept[None, :]
    source = jnp.max(jnp.where(before, at[None, :], -1), 1)
    hot = source[:, None] == at[None, :]
    return jnp.sum(jnp.where(hot, values[None, :], 0), 1).astype(jnp.int32)


def routing(mapping, local_blocks, row_count, capacity, row_rank):
    child_blocks = mapping.shape[0]
    at = jnp.arange(child_blocks, dtype=jnp.int32)
    owner = mapping // local_blocks
    target = mapping % local_blocks
    same = owner[:, None] == owner[None, :]
    rank = jnp.sum((same & (at[None, :] < at[:, None])).astype(jnp.int32), 1)
    slot = owner * capacity + rank
    slots = jnp.arange(row_count * capacity, dtype=jnp.int32)
    hit = slots[:, None] == slot[None, :]
    block_at = jnp.sum(jnp.where(hit, at[None, :], 0), 1).astype(jnp.int32)
    sent = last_kept(block_at, jnp.any(hit, 1))
    mine = owner == row_rank
    rows = jnp.arange(local_blocks, dtype=jnp.int32)
    at_row = (rows[:, None] == target[None, :]) & mine[None, :]
    used = jnp.any(at_row, 1)
    slot_of = last_kept(jnp.sum(jnp.where(at_row, rank[None, :], 0), 1).astype(jnp.int32), used)
    local = jnp.arange(capacity, dtype=jnp.int32)
    at_slot = (local[:, None] == rank[None, :]) & mine[None, :]
    filled = jnp.any(at_slot, 1)
    row_of = last_kept(jnp.sum(jnp.where(at_slot, target[None, :], 0), 1).astype(jnp.int32), filled)
    from_slot = last_kept(local, filled)
    return sent, (slot_of, used.astype(jnp.int32)), jnp.stack([row_of, filled.astype(jnp.int32), from_slot])


def down_the_rows(own, root, row_rank, row_count):
    kept = jnp.where(row_rank == root, own, 0)
    right = own
    for k in range(root, row_count - 1):
        right = lax.ppermute(right, "row", [(k, k + 1)])
        kept = kept + right
    left = own
    for k in range(root, 0, -1):
        left = lax.ppermute(left, "row", [(k, k - 1)])
        kept = kept + left
    return kept


def per_device(front_panel, front_slab, child_one, child_two, map_one, map_two):
    rows_dev, slab_width = front_slab.shape
    panel_width = front_panel.shape[1]
    child_blocks = map_one.shape[0]
    child_local = child_one.shape[0]
    row_count = lax.axis_size("row")
    col_count = lax.axis_size("col")
    row_rank = lax.axis_index("row")
    col_rank = lax.axis_index("col")
    piece = slab_width // row_count
    local_blocks = rows_dev // BLK
    capacity = 2 * child_blocks // row_count
    head = 2 * P_SIZE
    panel = front_panel.T

    top = sum(
        (lax.ppermute(panel[:, :head], "row", [(0, k)]) for k in range(1, row_count)),
        jnp.where(row_rank == 0, panel[:, :head], 0),
    )
    top = lax.all_gather(top, "col", axis=0, tiled=True)

    segments = []
    wanted_stop = head + col_count * slab_width
    for root in range(row_count):
        low = max(head, root * rows_dev) - root * rows_dev
        high = min(wanted_stop, (root + 1) * rows_dev) - root * rows_dev
        if high > low:
            segments.append(down_the_rows(panel[:, low:high], root, row_rank, row_count))
    wanted = jnp.concatenate(segments, 1)
    wanted = lax.all_to_all(wanted, "col", split_axis=1, concat_axis=0, tiled=True)

    sent_one, (slot_one, used_one), _ = routing(map_one, local_blocks, row_count, capacity, row_rank)
    sent_two, _, place_two = routing(map_two, local_blocks, row_count, capacity, row_rank)

    def split_columns(child):
        pieces = child.reshape(child_local, col_count, piece)
        return lax.all_to_all(pieces, "col", split_axis=1, concat_axis=0, tiled=True)

    def send_rows(received, sent):
        packed = pack_blocks(sent, received.reshape(child_blocks, BLK, piece))
        packed = packed.reshape(row_count, capacity, BLK, piece)
        return lax.all_to_all(packed, "row", split_axis=0, concat_axis=0, tiled=True)

    got_one = split_columns(child_one)
    arrived_one = send_rows(got_one, sent_one)
    got_two = split_columns(child_two)
    arrived_two = send_rows(got_two, sent_two)

    gathered = lax.all_gather(panel, "col", axis=0, tiled=True)

    inv_high, inv_low = factor_inverse(top)
    b_high, b_low = slab_rows(inv_high, inv_low, wanted)
    f_high, f_low, own = panel_rows(inv_high, inv_low, gathered, col_rank.reshape(1).astype(jnp.int32), panel_width)
    skipped = jnp.clip(head // BLK - row_rank * local_blocks, 0, local_blocks)
    table = jnp.stack([slot_one, used_one, jnp.broadcast_to(skipped, slot_one.shape).astype(jnp.int32)])
    slab = update_slab(table, f_high, f_low, b_high, b_low, front_slab, arrived_one)
    slab = place_child(place_two, arrived_two, slab)
    return (own.T, slab)


def solution(mesh):
    in_specs = (P("row", "col"), P("row", "col"), P("col", "row"), P("col", "row"), P(), P())
    out_specs = (P("row", "col"), P("row", "col"))
    return jax.shard_map(
        per_device, mesh=mesh, in_specs=in_specs, out_specs=out_specs, check_vma=False
    )
```

```python
import functools

import jax
import jax.numpy as jnp
from jax import lax
from jax.experimental import pallas as pl
from jax.experimental.pallas import tpu as pltpu
from jax.sharding import PartitionSpec as P


P_SIZE = 256
BLK = 256
SUB = 32
GROUP = 4
VMEM_BYTES = 56 * 1024 * 1024


def split_pair(value):
    high = value.astype(jnp.bfloat16)
    low = (value - high.astype(jnp.float32)).astype(jnp.bfloat16)
    return high, low


def dot3(a_high, a_low, b_high, b_low):
    def one(x, y):
        return jnp.dot(x, y, preferred_element_type=jnp.float32)

    return one(a_high, b_high) + (one(a_low, b_high) + one(a_high, b_low))


def exact_dot(a, b, contract):
    return lax.dot_general(
        a,
        b,
        (contract, ((), ())),
        precision=lax.Precision.HIGHEST,
        preferred_element_type=jnp.float32,
    )


def block_inverse(block):
    rows = lax.broadcasted_iota(jnp.int32, (SUB, SUB), 0)
    cols = lax.broadcasted_iota(jnp.int32, (SUB, SUB), 1)
    unit = (rows == cols).astype(jnp.float32)
    both = jnp.concatenate([block, unit, jnp.zeros((SUB, 128 - 2 * SUB), jnp.float32)], 1)
    row_of = lax.broadcasted_iota(jnp.int32, (SUB, 128), 0)
    scale = jnp.zeros((SUB, 128), jnp.float32)
    for j in range(0, SUB, GROUP):
        spread = [jnp.broadcast_to(both[:, j + k : j + k + 1], (SUB, 128)) for k in range(GROUP)]
        for k in range(GROUP):
            row = j + k
            pivot = jnp.broadcast_to(spread[k][row : row + 1, :], (SUB, 128))
            scale = jnp.where(row_of == row, pivot, scale)
            factor = jnp.where(row_of > row, spread[k] * (1.0 / pivot), 0.0)
            for m in range(k + 1, GROUP):
                spread[m] = spread[m] - factor * spread[m][row : row + 1, :]
            both = both - factor * both[row : row + 1, :]
    return (both / jnp.sqrt(scale))[:, SUB : 2 * SUB]


def inverse_steps(work_ref, first, last):
    size = work_ref.shape[0]
    for start in range(first, last, SUB):
        stop = start + SUB
        inverse = block_inverse(work_ref[start:stop, start:stop])
        lanes = lax.broadcasted_iota(jnp.int32, (SUB, size), 1)
        inside = (lanes >= start) & (lanes < stop)
        rows = exact_dot(inverse, jnp.where(inside, 0.0, work_ref[start:stop, :]), ((1,), (0,)))
        wide = jnp.concatenate([inverse] * (128 // SUB), 1)
        wide = jnp.concatenate([wide] * (size // 128), 1)
        rows = jnp.where(inside, wide, rows)
        if stop < size:
            below = exact_dot(work_ref[stop:size, start:stop], inverse, ((1,), (1,)))
            lanes_b = lax.broadcasted_iota(jnp.int32, (size - stop, size), 1)
            inside_b = (lanes_b >= start) & (lanes_b < stop)
            kept = jnp.where(inside_b, 0.0, work_ref[stop:size, :])
            work_ref[stop:size, :] = kept - exact_dot(below, rows, ((1,), (0,)))
        work_ref[start:stop, :] = jnp.where(lanes < stop, rows, 0.0)


def first_half_kernel(rank_ref, *refs):
    parts, work_ref = refs[:-1], refs[-1]
    height = parts[0].shape[0]
    for far, part in enumerate(parts):
        start = jnp.bitwise_xor(rank_ref[0], far) * height
        work_ref[pl.ds(pl.multiple_of(start, 8), height), :] = part[...]
    inverse_steps(work_ref, 0, P_SIZE)


def second_half_kernel(half_ref, high_ref, low_ref, work_ref):
    work_ref[...] = half_ref[...]
    inverse_steps(work_ref, P_SIZE, half_ref.shape[0])
    high, low = split_pair(work_ref[...])
    high_ref[...] = high
    low_ref[...] = low


def factor_first(rank, parts):
    size = parts[0].shape[1]
    return pl.pallas_call(
        first_half_kernel,
        in_specs=[pl.BlockSpec(memory_space=pltpu.SMEM)] + [pl.BlockSpec(memory_space=pltpu.VMEM)] * len(parts),
        out_shape=jax.ShapeDtypeStruct((size, size), jnp.float32),
        compiler_params=pltpu.CompilerParams(vmem_limit_bytes=VMEM_BYTES),
        cost_estimate=pl.CostEstimate(flops=size * size * 60000, transcendentals=0, bytes_accessed=2 * size * size * 4),
        name="factor_first",
    )(rank, *parts)


def factor_second(half):
    size = half.shape[0]
    pair = jax.ShapeDtypeStruct((size, size), jnp.bfloat16)
    return pl.pallas_call(
        second_half_kernel,
        out_shape=(pair, pair),
        scratch_shapes=[pltpu.VMEM((size, size), jnp.float32)],
        compiler_params=pltpu.CompilerParams(vmem_limit_bytes=VMEM_BYTES),
        cost_estimate=pl.CostEstimate(flops=size * size * 60000, transcendentals=0, bytes_accessed=2 * size * size * 4),
        name="factor_second",
    )(half)


def panel_kernel(rank_ref, high_ref, low_ref, panel_ref, fhigh_ref, flow_ref, own_ref, work_ref):
    p_high, p_low = split_pair(panel_ref[...])
    work_ref[...] = dot3(high_ref[...], low_ref[...], p_high, p_low)
    own = own_ref.shape[0]
    own_ref[...] = work_ref[pl.ds(pl.multiple_of(rank_ref[0] * own, 8), own), :]
    f_high, f_low = split_pair(work_ref[...].T)
    fhigh_ref[...] = f_high
    flow_ref[...] = f_low


def panel_rows(high, low, gathered, rank, own):
    size, rows = gathered.shape
    tile = 512
    pair = jax.ShapeDtypeStruct((rows, size), jnp.bfloat16)
    return pl.pallas_call(
        panel_kernel,
        grid_spec=pltpu.PrefetchScalarGridSpec(
            num_scalar_prefetch=1,
            grid=(rows // tile,),
            in_specs=[
                pl.BlockSpec((size, size), lambda i, r: (0, 0)),
                pl.BlockSpec((size, size), lambda i, r: (0, 0)),
                pl.BlockSpec((size, tile), lambda i, r: (0, i)),
            ],
            out_specs=[
                pl.BlockSpec((tile, size), lambda i, r: (i, 0)),
                pl.BlockSpec((tile, size), lambda i, r: (i, 0)),
                pl.BlockSpec((own, tile), lambda i, r: (0, i)),
            ],
            scratch_shapes=[pltpu.VMEM((size, tile), jnp.float32)],
        ),
        out_shape=(pair, pair, jax.ShapeDtypeStruct((own, rows), jnp.float32)),
        compiler_params=pltpu.CompilerParams(vmem_limit_bytes=VMEM_BYTES),
        cost_estimate=pl.CostEstimate(flops=6 * rows * size * size, transcendentals=0, bytes_accessed=8 * rows * size),
        name="panel_rows",
    )(rank, high, low, gathered)


def slab_rows_kernel(rank_ref, high_ref, low_ref, *refs):
    parts = refs[:-3]
    bhigh_ref, blow_ref, work_ref = refs[-3:]
    height = parts[0].shape[0]
    for far, part in enumerate(parts):
        start = jnp.bitwise_xor(rank_ref[0], far) * height
        work_ref[pl.ds(pl.multiple_of(start, 8), height), :] = part[...]
    p_high, p_low = split_pair(work_ref[...])
    b_high, b_low = split_pair(dot3(high_ref[...], low_ref[...], p_high, p_low))
    bhigh_ref[...] = b_high
    blow_ref[...] = b_low


def slab_rows(rank, high, low, parts):
    size = high.shape[0]
    height, rows = parts[0].shape
    tile = 512
    pair = jax.ShapeDtypeStruct((size, rows), jnp.bfloat16)
    whole = pl.BlockSpec((size, size), lambda i, r: (0, 0))
    out = pl.BlockSpec((size, tile), lambda i, r: (0, i))
    return pl.pallas_call(
        slab_rows_kernel,
        grid_spec=pltpu.PrefetchScalarGridSpec(
            num_scalar_prefetch=1,
            grid=(rows // tile,),
            in_specs=[whole, whole] + [pl.BlockSpec((height, tile), lambda i, r: (0, i))] * len(parts),
            out_specs=[out, out],
            scratch_shapes=[pltpu.VMEM((size, tile), jnp.float32)],
        ),
        out_shape=(pair, pair),
        compiler_params=pltpu.CompilerParams(vmem_limit_bytes=VMEM_BYTES),
        cost_estimate=pl.CostEstimate(flops=6 * rows * size * size, transcendentals=0, bytes_accessed=8 * rows * size),
        name="slab_rows",
    )(rank, high, low, *parts)


def add_stacked(block, out_ref):
    count, _, _, piece = block.shape
    for a in range(count):
        cols = slice(a * piece, (a + 1) * piece)
        out_ref[:, cols] = out_ref[:, cols] + block[a, 0].astype(jnp.float32)


def add_around(rank, pieces, out_ref):
    count = len(pieces)
    piece = pieces[0].shape[2]

    def add(part, cols):
        out_ref[:, cols] = out_ref[:, cols] + part[0].astype(jnp.float32)

    for far in range(count):
        source = lax.rem(rank + count - far, count)
        if piece % 128 == 0:
            add(pieces[far], pl.ds(pl.multiple_of(source * piece, 128), piece))
        else:
            for a in range(count):
                pl.when(source == a)(functools.partial(add, pieces[far], slice(a * piece, (a + 1) * piece)))


def update_kernel(first, skip_ref, fhigh_ref, flow_ref, bhigh_ref, blow_ref, slab_ref, *refs):
    out_ref = refs[-1]
    step = pl.program_id(0) + first

    @pl.when(step < skip_ref[0])
    def _():
        out_ref[...] = slab_ref[...]

    @pl.when(step >= skip_ref[0])
    def _():
        out_ref[...] = slab_ref[...] - dot3(fhigh_ref[...], flow_ref[...], bhigh_ref[...], blow_ref[...])


def update_slab(skipped, f_high, f_low, b_high, b_low, slab, done, first):
    rows, width = slab.shape
    part, size = f_high.shape
    rowspec = pl.BlockSpec((BLK, size), lambda i, t: (i, 0))
    bspec = pl.BlockSpec((size, width), lambda i, t: (0, 0))
    tile = pl.BlockSpec((BLK, width), lambda i, t: (i + first, 0))
    before = [] if done is None else [done]
    return pl.pallas_call(
        functools.partial(update_kernel, first),
        grid_spec=pltpu.PrefetchScalarGridSpec(
            num_scalar_prefetch=1,
            grid=(part // BLK,),
            in_specs=[rowspec, rowspec, bspec, bspec, tile] + [pl.BlockSpec(memory_space=pl.ANY)] * len(before),
            out_specs=tile,
        ),
        out_shape=jax.ShapeDtypeStruct((rows, width), jnp.float32),
        input_output_aliases={6: 0} if before else {},
        compiler_params=pltpu.CompilerParams(vmem_limit_bytes=VMEM_BYTES),
        cost_estimate=pl.CostEstimate(flops=6 * part * size * width, transcendentals=0, bytes_accessed=8 * part * width),
        name="update_slab",
    )(skipped, f_high, f_low, b_high, b_low, slab, *before)


def place_kernel(rank_ref, rows_ref, valid_ref, slot_ref, *refs):
    pieces = refs[:-2]
    slab_ref, out_ref = refs[-2:]
    step = pl.program_id(0)
    first = (step == 0) | (rows_ref[step] != rows_ref[jnp.maximum(step - 1, 0)])

    @pl.when(first)
    def _():
        out_ref[...] = slab_ref[...]

    @pl.when(valid_ref[step] > 0)
    def _():
        if len(pieces) == 1:
            add_stacked(pieces[0], out_ref)
        else:
            add_around(rank_ref[0], pieces, out_ref)


def place_blocks(rank, lists, pieces, slab):
    rows, width = slab.shape
    tile = pl.BlockSpec((BLK, width), lambda i, k, t, v, s: (t[i], 0))
    if len(pieces) == 1:
        count, slots, _, piece = pieces[0].shape
        part = pl.BlockSpec((count, 1, BLK, piece), lambda i, k, t, v, s: (0, s[i], 0, 0))
    else:
        slots, _, piece = pieces[0].shape
        part = pl.BlockSpec((1, BLK, piece), lambda i, k, t, v, s: (s[i], 0, 0))
    return pl.pallas_call(
        place_kernel,
        grid_spec=pltpu.PrefetchScalarGridSpec(
            num_scalar_prefetch=4,
            grid=(slots,),
            in_specs=[part] * len(pieces) + [tile],
            out_specs=tile,
        ),
        out_shape=jax.ShapeDtypeStruct((rows, width), jnp.float32),
        input_output_aliases={4 + len(pieces): 0},
        compiler_params=pltpu.CompilerParams(vmem_limit_bytes=VMEM_BYTES),
        cost_estimate=pl.CostEstimate(flops=0, transcendentals=0, bytes_accessed=8 * slots * BLK * width),
        name="place_blocks",
    )(rank, *lists, *pieces, slab)


def copy_all(copies):
    copies = list(copies)
    for copy in copies:
        copy.start()
    for copy in copies:
        copy.wait()


def split_columns(children, count):
    rows, width = children[0].shape
    piece = width // count
    if piece % 128:
        return jnp.stack([child.reshape(rows, count, piece).transpose(1, 0, 2) for child in children], 1)

    def kernel(*refs):
        sources, out, sems = refs[:-2], refs[-2], refs[-1]
        copy_all(
            pltpu.make_async_copy(source.at[:, b * piece : (b + 1) * piece], out.at[b, n], sems.at[n, b])
            for n, source in enumerate(sources)
            for b in range(count)
        )

    return pl.pallas_call(
        kernel,
        in_specs=[pl.BlockSpec(memory_space=pltpu.VMEM)] * len(children),
        out_specs=pl.BlockSpec(memory_space=pl.ANY),
        out_shape=jax.ShapeDtypeStruct((count, len(children), rows, piece), children[0].dtype),
        scratch_shapes=[pltpu.SemaphoreType.DMA((len(children), count))],
        cost_estimate=pl.CostEstimate(flops=0, transcendentals=0, bytes_accessed=8 * rows * width),
        compiler_params=pltpu.CompilerParams(vmem_limit_bytes=VMEM_BYTES),
        name="split_columns",
    )(*children)


def gather_blocks(table, blocks, groups, size):
    _, height, piece = blocks.shape

    def kernel(table_ref, source, *refs):
        outs, sems = refs[:-1], refs[-1]
        copy_all(
            [
                pltpu.make_async_copy(
                    source.at[table_ref[g * size + n]], outs[g].at[n], sems.at[g * size + n]
                )
                for g in range(groups)
                for n in range(size)
            ]
        )

    anyspec = pl.BlockSpec(memory_space=pl.ANY)
    return pl.pallas_call(
        kernel,
        grid_spec=pltpu.PrefetchScalarGridSpec(
            num_scalar_prefetch=1,
            grid=(1,),
            in_specs=[pl.BlockSpec(blocks.shape, lambda i, t: (0, 0, 0))],
            out_specs=[anyspec] * groups,
            scratch_shapes=[pltpu.SemaphoreType.DMA((groups * size,))],
        ),
        out_shape=[jax.ShapeDtypeStruct((size, height, piece), blocks.dtype)] * groups,
        cost_estimate=pl.CostEstimate(flops=0, transcendentals=0, bytes_accessed=4 * groups * size * height * piece),
        compiler_params=pltpu.CompilerParams(vmem_limit_bytes=VMEM_BYTES),
        name="gather_blocks",
    )(table, blocks)


def routing_tables(maps, rank, row_count, local_blocks, per_source, base, extra):
    children = len(maps)
    blocks = maps[0].shape[0]
    sent_base = row_count * children * base
    sent_extra = children * row_count * extra
    lists = [children * base] + [max(extra, 1)] * children
    shapes = [(max(sent_base, 1),), (max(sent_extra, 1),)]
    for size in lists:
        shapes += [(size,)] * 3
    shapes.append((1,))

    def kernel(rank_ref, *refs):
        map_refs = refs[:children]
        base_ref, extra_ref = refs[children : children + 2]
        outs = refs[children + 2 : children + 2 + 3 * len(lists)]
        state_ref = refs[children + 2 + 3 * len(lists)]
        counts, where = refs[-2:]
        mine = rank_ref[0]

        def clear(ref, size, value):
            def body(i, _):
                ref[i] = jnp.int32(value)
                return 0

            lax.fori_loop(0, size, body, 0)

        clear(base_ref, shapes[0][0], 0)
        clear(extra_ref, shapes[1][0], 0)
        clear(counts, children * row_count, 0)
        clear(where, children * local_blocks, -1)
        for c in range(children):

            def body(i, _, c=c):
                value = map_refs[c][i]
                owner = value // local_blocks
                far = lax.rem(owner + row_count - mine, row_count)
                at = counts[c * row_count + owner]
                counts[c * row_count + owner] = at + 1
                block = (i // per_source) * (children * per_source) + c * per_source + lax.rem(i, per_source)

                @pl.when(at < base)
                def _():
                    base_ref[(far * children + c) * base + at] = block

                if extra:

                    @pl.when(at >= base)
                    def _():
                        extra_ref[(c * row_count + far) * extra + at - base] = block

                @pl.when(owner == mine)
                def _():
                    where[c * local_blocks + value - owner * local_blocks] = at

                return 0

            lax.fori_loop(0, blocks, body, 0)

        def listed(out, size, chosen):
            rows_ref, valid_ref, slot_ref = out

            def put(at, row, slot):
                rows_ref[at] = row
                valid_ref[at] = jnp.int32(1)
                slot_ref[at] = slot
                return at + 1

            def body(t, at):
                for c, low, high, shift in chosen:
                    slot = where[c * local_blocks + t]
                    hit = (slot >= low) & (slot < high)

                    @pl.when(hit)
                    def _(at=at, slot=slot, low=low, shift=shift):
                        put(at, t, slot - low + shift)

                    at = at + hit.astype(jnp.int32)
                return at

            filled = lax.fori_loop(0, local_blocks, body, jnp.int32(0))
            last = jnp.maximum(filled - 1, 0)
            row = jnp.where(filled > 0, rows_ref[last], 0)
            slot = jnp.where(filled > 0, slot_ref[last], 0)

            def pad(i, _):
                @pl.when(i >= filled)
                def _():
                    rows_ref[i] = row
                    valid_ref[i] = jnp.int32(0)
                    slot_ref[i] = slot

                return 0

            lax.fori_loop(0, size, pad, 0)

        for n, size in enumerate(lists):
            out = outs[3 * n : 3 * n + 3]
            clear(out[0], size, 0)
            clear(out[2], size, 0)
            if n == 0:
                chosen = [(c, 0, base, c * base) for c in range(children)]
            else:
                chosen = [(n - 1, base, base + extra, 0)]
            listed(out, size, chosen)

        state = jnp.int32(0)
        for c in range(children):
            busy = jnp.int32(0)
            over = jnp.int32(0)
            for k in range(row_count):
                more = counts[c * row_count + k] > base
                busy = jnp.where(more, k, busy)
                over = over + more.astype(jnp.int32)
            state = state * (row_count + 1) + jnp.where(over > 1, row_count, busy)
        state_ref[0] = state

    smem = pl.BlockSpec(memory_space=pltpu.SMEM)
    return pl.pallas_call(
        kernel,
        in_specs=[smem] * (1 + children),
        out_specs=[smem] * len(shapes),
        out_shape=[jax.ShapeDtypeStruct(shape, jnp.int32) for shape in shapes],
        scratch_shapes=[
            pltpu.SMEM((children * row_count,), jnp.int32),
            pltpu.SMEM((children * local_blocks,), jnp.int32),
        ],
        name="routing_tables",
    )(rank, *maps)


def down_the_rows(own, root, row_rank, row_count):
    kept = jnp.where(row_rank == root, own, 0)
    for step in (1, -1):
        moving, k, hop = own, root, 1
        while 0 <= k + step < row_count:
            moving = lax.ppermute(moving, "row", [(k, k + step)])
            kept = kept + moving
            k += step
            hop += 1
    return kept


def around(value, far, row_count):
    return lax.ppermute(value, "row", [(k, (k + far) % row_count) for k in range(row_count)])


def extra_exchange(state, groups, row_count):
    def branch(code):
        choices = []
        for _ in groups:
            choices.append(code % (row_count + 1))
            code //= row_count + 1
        choices = choices[::-1]

        def run(*flat):
            got = []
            for c, owner in enumerate(choices):
                for far in range(1, row_count):
                    value = flat[c * (row_count - 1) + far - 1]
                    if owner == row_count:
                        got.append(around(value, far, row_count))
                    else:
                        got.append(lax.ppermute(value, "row", [((owner - far) % row_count, owner)]))
            return tuple(got)

        return run

    flat = [value for group in groups for value in group[1:]]
    branches = [branch(code) for code in range((row_count + 1) ** len(groups))]
    got = lax.switch(state, branches, *flat)
    step = row_count - 1
    return [[group[0], *got[c * step : (c + 1) * step]] for c, group in enumerate(groups)]


def per_device(front_panel, front_slab, child_one, child_two, map_one, map_two):
    rows_dev, slab_width = front_slab.shape
    panel_width = front_panel.shape[1]
    child_blocks = map_one.shape[0]
    row_count = lax.axis_size("row")
    col_count = lax.axis_size("col")
    row_rank = lax.axis_index("row").astype(jnp.int32)
    col_rank = lax.axis_index("col").astype(jnp.int32)
    local_blocks = rows_dev // BLK
    capacity = 2 * child_blocks // row_count
    base = capacity // 2 if row_count <= 4 else capacity
    extra = capacity - base
    head = 2 * P_SIZE
    panel = front_panel.T
    piece = slab_width // row_count

    def spread(value):
        return [value] + [
            lax.ppermute(value, "col", [(k, k ^ far) for k in range(col_count)]) for far in range(1, col_count)
        ]

    pieces = split_columns((child_one, child_two), col_count)
    panel, pieces = lax.optimization_barrier((panel, pieces))
    got = lax.all_to_all(pieces, "col", split_axis=0, concat_axis=0, tiled=True)
    got = got.reshape(2 * child_blocks, BLK, piece)

    top = sum(
        (lax.ppermute(panel[:, :head], "row", [(0, k)]) for k in range(1, row_count)),
        jnp.where(row_rank == 0, panel[:, :head], 0),
    )
    even = col_count & (col_count - 1) == 0
    part_rank = col_rank.reshape(1) if even else jnp.zeros((1,), jnp.int32)
    top_parts = spread(top) if even else [lax.all_gather(top, "col", axis=0, tiled=True)]

    segments = []
    wanted_stop = head + col_count * slab_width
    for root in range(row_count):
        low = max(head, root * rows_dev) - root * rows_dev
        high = min(wanted_stop, (root + 1) * rows_dev) - root * rows_dev
        if high > low:
            segments.append(down_the_rows(panel[:, low:high], root, row_rank, row_count))
    wanted = jnp.concatenate(segments, 1)

    rank = row_rank.reshape(1)
    tables = routing_tables(
        (map_one, map_two), rank, row_count, local_blocks, child_one.shape[0] // BLK, base, extra
    )
    base_table, extra_table = tables[:2]
    lists = [tables[2 + 3 * n : 5 + 3 * n] for n in range(3)]
    state = tables[11][0]
    sent = gather_blocks(base_table, got, row_count, 2 * base)
    arrived = [sent[0]]
    for far in range(1, row_count):
        arrived.append(around(sent[far], far, row_count))

    parts = 2 if rows_dev % (2 * 512) == 0 else 1
    part = rows_dev // parts
    panel_later, got = lax.optimization_barrier((panel, got))
    gathered = [
        lax.all_gather(panel_later[:, n * part : (n + 1) * part], "col", axis=0, tiled=True)
        for n in range(parts)
    ]
    wanted = lax.all_to_all(wanted, "col", split_axis=1, concat_axis=0, tiled=True)

    half = factor_first(part_rank, top_parts)
    inv_high, inv_low = factor_second(half)
    b_high, b_low = slab_rows(jnp.zeros((1,), jnp.int32), inv_high, inv_low, [wanted])
    skipped = jnp.clip(head // BLK - row_rank * local_blocks, 0, local_blocks).reshape(1)
    owns, slab = [], None
    for n in range(parts):
        f_high, f_low, own = panel_rows(inv_high, inv_low, gathered[n], col_rank.reshape(1), panel_width)
        owns.append(own)
        slab = update_slab(skipped, f_high, f_low, b_high, b_low, front_slab, slab, n * part // BLK)
    own = jnp.concatenate(owns, 1)
    slab = place_blocks(rank, lists[0], arrived, slab)
    if extra:
        groups = gather_blocks(extra_table, got, 2 * row_count, extra)
        groups, slab = lax.optimization_barrier((groups, slab))
        groups = extra_exchange(state, [groups[:row_count], groups[row_count:]], row_count)
        slab = place_blocks(rank, lists[1], groups[0], slab)
        slab = place_blocks(rank, lists[2], groups[1], slab)
    return (own.T, slab)


def solution(mesh):
    in_specs = (P("row", "col"), P("row", "col"), P("col", "row"), P("col", "row"), P(), P())
    out_specs = (P("row", "col"), P("row", "col"))
    return jax.shard_map(per_device, mesh=mesh, in_specs=in_specs, out_specs=out_specs, check_vma=False)
```

```python
import functools

import jax
import jax.numpy as jnp
from jax import lax
from jax.experimental import pallas as pl
from jax.experimental.pallas import tpu as pltpu
from jax.sharding import PartitionSpec as P


P_SIZE = 256
BLK = 256
SUB = 32
GROUP = 4
VMEM_BYTES = 56 * 1024 * 1024


def split_pair(value):
    high = value.astype(jnp.bfloat16)
    low = (value - high.astype(jnp.float32)).astype(jnp.bfloat16)
    return high, low


def dot3(a_high, a_low, b_high, b_low):
    def one(x, y):
        return jnp.dot(x, y, preferred_element_type=jnp.float32)

    return one(a_high, b_high) + (one(a_low, b_high) + one(a_high, b_low))


def exact_dot(a, b, contract):
    return lax.dot_general(
        a,
        b,
        (contract, ((), ())),
        precision=lax.Precision.HIGHEST,
        preferred_element_type=jnp.float32,
    )


def block_inverse(block):
    rows = lax.broadcasted_iota(jnp.int32, (SUB, SUB), 0)
    cols = lax.broadcasted_iota(jnp.int32, (SUB, SUB), 1)
    unit = (rows == cols).astype(jnp.float32)
    both = jnp.concatenate([block, unit, jnp.zeros((SUB, 128 - 2 * SUB), jnp.float32)], 1)
    row_of = lax.broadcasted_iota(jnp.int32, (SUB, 128), 0)
    scale = jnp.zeros((SUB, 128), jnp.float32)
    for j in range(0, SUB, GROUP):
        spread = [jnp.broadcast_to(both[:, j + k : j + k + 1], (SUB, 128)) for k in range(GROUP)]
        for k in range(GROUP):
            row = j + k
            pivot = jnp.broadcast_to(spread[k][row : row + 1, :], (SUB, 128))
            scale = jnp.where(row_of == row, pivot, scale)
            factor = jnp.where(row_of > row, spread[k] * (1.0 / pivot), 0.0)
            for m in range(k + 1, GROUP):
                spread[m] = spread[m] - factor * spread[m][row : row + 1, :]
            both = both - factor * both[row : row + 1, :]
    return (both / jnp.sqrt(scale))[:, SUB : 2 * SUB]


def inverse_steps(work_ref, first, last):
    size = work_ref.shape[0]
    for start in range(first, last, SUB):
        stop = start + SUB
        inverse = block_inverse(work_ref[start:stop, start:stop])
        lanes = lax.broadcasted_iota(jnp.int32, (SUB, size), 1)
        inside = (lanes >= start) & (lanes < stop)
        rows = exact_dot(inverse, jnp.where(inside, 0.0, work_ref[start:stop, :]), ((1,), (0,)))
        wide = jnp.concatenate([inverse] * (128 // SUB), 1)
        wide = jnp.concatenate([wide] * (size // 128), 1)
        rows = jnp.where(inside, wide, rows)
        if stop < size:
            below = exact_dot(work_ref[stop:size, start:stop], inverse, ((1,), (1,)))
            lanes_b = lax.broadcasted_iota(jnp.int32, (size - stop, size), 1)
            inside_b = (lanes_b >= start) & (lanes_b < stop)
            kept = jnp.where(inside_b, 0.0, work_ref[stop:size, :])
            work_ref[stop:size, :] = kept - exact_dot(below, rows, ((1,), (0,)))
        work_ref[start:stop, :] = jnp.where(lanes < stop, rows, 0.0)


def first_half_kernel(rank_ref, *refs):
    parts, work_ref = refs[:-1], refs[-1]
    height = parts[0].shape[0]
    for far, part in enumerate(parts):
        start = jnp.bitwise_xor(rank_ref[0], far) * height
        work_ref[pl.ds(pl.multiple_of(start, 8), height), :] = part[...]
    inverse_steps(work_ref, 0, P_SIZE)


def second_half_kernel(half_ref, high_ref, low_ref, work_ref):
    work_ref[...] = half_ref[...]
    inverse_steps(work_ref, P_SIZE, half_ref.shape[0])
    high, low = split_pair(work_ref[...])
    high_ref[...] = high
    low_ref[...] = low


def factor_first(rank, parts):
    size = parts[0].shape[1]
    return pl.pallas_call(
        first_half_kernel,
        in_specs=[pl.BlockSpec(memory_space=pltpu.SMEM)] + [pl.BlockSpec(memory_space=pltpu.VMEM)] * len(parts),
        out_shape=jax.ShapeDtypeStruct((size, size), jnp.float32),
        compiler_params=pltpu.CompilerParams(vmem_limit_bytes=VMEM_BYTES),
        cost_estimate=pl.CostEstimate(flops=size * size * 60000, transcendentals=0, bytes_accessed=2 * size * size * 4),
        name="factor_first",
    )(rank, *parts)


def factor_second(half):
    size = half.shape[0]
    pair = jax.ShapeDtypeStruct((size, size), jnp.bfloat16)
    return pl.pallas_call(
        second_half_kernel,
        out_shape=(pair, pair),
        scratch_shapes=[pltpu.VMEM((size, size), jnp.float32)],
        compiler_params=pltpu.CompilerParams(vmem_limit_bytes=VMEM_BYTES),
        cost_estimate=pl.CostEstimate(flops=size * size * 60000, transcendentals=0, bytes_accessed=2 * size * size * 4),
        name="factor_second",
    )(half)


def panel_kernel(rank_ref, high_ref, low_ref, panel_ref, fhigh_ref, flow_ref, own_ref, work_ref):
    p_high, p_low = split_pair(panel_ref[...])
    work_ref[...] = dot3(high_ref[...], low_ref[...], p_high, p_low)
    own = own_ref.shape[0]
    own_ref[...] = work_ref[pl.ds(pl.multiple_of(rank_ref[0] * own, 8), own), :]
    f_high, f_low = split_pair(work_ref[...].T)
    fhigh_ref[...] = f_high
    flow_ref[...] = f_low


def panel_rows(high, low, gathered, rank, own):
    size, rows = gathered.shape
    tile = 512
    pair = jax.ShapeDtypeStruct((rows, size), jnp.bfloat16)
    return pl.pallas_call(
        panel_kernel,
        grid_spec=pltpu.PrefetchScalarGridSpec(
            num_scalar_prefetch=1,
            grid=(rows // tile,),
            in_specs=[
                pl.BlockSpec((size, size), lambda i, r: (0, 0)),
                pl.BlockSpec((size, size), lambda i, r: (0, 0)),
                pl.BlockSpec((size, tile), lambda i, r: (0, i)),
            ],
            out_specs=[
                pl.BlockSpec((tile, size), lambda i, r: (i, 0)),
                pl.BlockSpec((tile, size), lambda i, r: (i, 0)),
                pl.BlockSpec((own, tile), lambda i, r: (0, i)),
            ],
            scratch_shapes=[pltpu.VMEM((size, tile), jnp.float32)],
        ),
        out_shape=(pair, pair, jax.ShapeDtypeStruct((own, rows), jnp.float32)),
        compiler_params=pltpu.CompilerParams(vmem_limit_bytes=VMEM_BYTES),
        cost_estimate=pl.CostEstimate(flops=6 * rows * size * size, transcendentals=0, bytes_accessed=8 * rows * size),
        name="panel_rows",
    )(rank, high, low, gathered)


def slab_rows_kernel(rank_ref, high_ref, low_ref, *refs):
    parts = refs[:-3]
    bhigh_ref, blow_ref, work_ref = refs[-3:]
    height = parts[0].shape[0]
    for far, part in enumerate(parts):
        start = jnp.bitwise_xor(rank_ref[0], far) * height
        work_ref[pl.ds(pl.multiple_of(start, 8), height), :] = part[...]
    p_high, p_low = split_pair(work_ref[...])
    b_high, b_low = split_pair(dot3(high_ref[...], low_ref[...], p_high, p_low))
    bhigh_ref[...] = b_high
    blow_ref[...] = b_low


def slab_rows(rank, high, low, parts):
    size = high.shape[0]
    height, rows = parts[0].shape
    tile = 512
    pair = jax.ShapeDtypeStruct((size, rows), jnp.bfloat16)
    whole = pl.BlockSpec((size, size), lambda i, r: (0, 0))
    out = pl.BlockSpec((size, tile), lambda i, r: (0, i))
    return pl.pallas_call(
        slab_rows_kernel,
        grid_spec=pltpu.PrefetchScalarGridSpec(
            num_scalar_prefetch=1,
            grid=(rows // tile,),
            in_specs=[whole, whole] + [pl.BlockSpec((height, tile), lambda i, r: (0, i))] * len(parts),
            out_specs=[out, out],
            scratch_shapes=[pltpu.VMEM((size, tile), jnp.float32)],
        ),
        out_shape=(pair, pair),
        compiler_params=pltpu.CompilerParams(vmem_limit_bytes=VMEM_BYTES),
        cost_estimate=pl.CostEstimate(flops=6 * rows * size * size, transcendentals=0, bytes_accessed=8 * rows * size),
        name="slab_rows",
    )(rank, high, low, *parts)


def add_stacked(block, out_ref):
    count, _, _, piece = block.shape
    for a in range(count):
        cols = slice(a * piece, (a + 1) * piece)
        out_ref[:, cols] = out_ref[:, cols] + block[a, 0].astype(jnp.float32)


def add_around(rank, pieces, out_ref):
    count = len(pieces)
    piece = pieces[0].shape[2]

    def add(part, cols):
        out_ref[:, cols] = out_ref[:, cols] + part[0].astype(jnp.float32)

    for far in range(count):
        source = lax.rem(rank + count - far, count)
        if piece % 128 == 0:
            add(pieces[far], pl.ds(pl.multiple_of(source * piece, 128), piece))
        else:
            for a in range(count):
                pl.when(source == a)(functools.partial(add, pieces[far], slice(a * piece, (a + 1) * piece)))


def update_kernel(first, groups, rank_ref, skip_ref, *refs):
    where, refs = refs[: 2 * groups], refs[2 * groups :]
    fhigh_ref, flow_ref, bhigh_ref, blow_ref, slab_ref = refs[:5]
    out_ref = refs[-1]
    step = pl.program_id(0) + first

    @pl.when(step < skip_ref[0])
    def _():
        out_ref[...] = slab_ref[...]

    @pl.when(step >= skip_ref[0])
    def _():
        out_ref[...] = slab_ref[...] - dot3(fhigh_ref[...], flow_ref[...], bhigh_ref[...], blow_ref[...])

    for c in range(groups):
        count = (len(refs) - 6) // groups
        pieces = refs[5 + c * count : 5 + (c + 1) * count]

        @pl.when(where[2 * c + 1][step] > 0)
        def _(pieces=pieces):
            add_around(rank_ref[0], pieces, out_ref)


def update_slab(rank, skipped, where, f_high, f_low, b_high, b_low, slab, groups, done, first):
    rows, width = slab.shape
    part, size = f_high.shape
    rowspec = pl.BlockSpec((BLK, size), lambda i, *t: (i, 0))
    bspec = pl.BlockSpec((size, width), lambda i, *t: (0, 0))
    tile = pl.BlockSpec((BLK, width), lambda i, *t: (i + first, 0))
    pieces, specs = [], []
    for c, group in enumerate(groups):
        piece = group[0].shape[2]
        pieces += group
        specs += [pl.BlockSpec((1, BLK, piece), lambda i, *t, c=c: (t[2 + 2 * c][i + first], 0, 0))] * len(group)
    before = [] if done is None else [done]
    kernel = functools.partial(update_kernel, first, len(groups))
    if before:
        inner = kernel

        def kernel(*refs):
            inner(*refs[:-2], refs[-1])

    return pl.pallas_call(
        kernel,
        grid_spec=pltpu.PrefetchScalarGridSpec(
            num_scalar_prefetch=2 + 2 * len(groups),
            grid=(part // BLK,),
            in_specs=[rowspec, rowspec, bspec, bspec, tile]
            + specs
            + [pl.BlockSpec(memory_space=pl.ANY)] * len(before),
            out_specs=tile,
        ),
        out_shape=jax.ShapeDtypeStruct((rows, width), jnp.float32),
        input_output_aliases={2 + 2 * len(groups) + 5 + len(pieces): 0} if before else {},
        compiler_params=pltpu.CompilerParams(vmem_limit_bytes=VMEM_BYTES),
        cost_estimate=pl.CostEstimate(flops=6 * part * size * width, transcendentals=0, bytes_accessed=8 * part * width),
        name="update_slab",
    )(rank, skipped, *where, f_high, f_low, b_high, b_low, slab, *pieces, *before)


def place_kernel(rank_ref, rows_ref, valid_ref, slot_ref, *refs):
    pieces = refs[:-2]
    slab_ref, out_ref = refs[-2:]
    step = pl.program_id(0)
    first = (step == 0) | (rows_ref[step] != rows_ref[jnp.maximum(step - 1, 0)])

    @pl.when(first)
    def _():
        out_ref[...] = slab_ref[...]

    @pl.when(valid_ref[step] > 0)
    def _():
        if len(pieces) == 1:
            add_stacked(pieces[0], out_ref)
        else:
            add_around(rank_ref[0], pieces, out_ref)


def place_blocks(rank, lists, pieces, slab):
    rows, width = slab.shape
    tile = pl.BlockSpec((BLK, width), lambda i, k, t, v, s: (t[i], 0))
    if len(pieces) == 1:
        count, slots, _, piece = pieces[0].shape
        part = pl.BlockSpec((count, 1, BLK, piece), lambda i, k, t, v, s: (0, s[i], 0, 0))
    else:
        slots, _, piece = pieces[0].shape
        part = pl.BlockSpec((1, BLK, piece), lambda i, k, t, v, s: (s[i], 0, 0))
    return pl.pallas_call(
        place_kernel,
        grid_spec=pltpu.PrefetchScalarGridSpec(
            num_scalar_prefetch=4,
            grid=(slots,),
            in_specs=[part] * len(pieces) + [tile],
            out_specs=tile,
        ),
        out_shape=jax.ShapeDtypeStruct((rows, width), jnp.float32),
        input_output_aliases={4 + len(pieces): 0},
        compiler_params=pltpu.CompilerParams(vmem_limit_bytes=VMEM_BYTES),
        cost_estimate=pl.CostEstimate(flops=0, transcendentals=0, bytes_accessed=8 * slots * BLK * width),
        name="place_blocks",
    )(rank, *lists, *pieces, slab)


def copy_all(copies):
    copies = list(copies)
    for copy in copies:
        copy.start()
    for copy in copies:
        copy.wait()


def split_columns(children, count):
    rows, width = children[0].shape
    piece = width // count
    if piece % 128:
        return jnp.stack([child.reshape(rows, count, piece).transpose(1, 0, 2) for child in children], 1)

    def kernel(*refs):
        sources, out, sems = refs[:-2], refs[-2], refs[-1]
        copy_all(
            pltpu.make_async_copy(source.at[:, b * piece : (b + 1) * piece], out.at[b, n], sems.at[n, b])
            for n, source in enumerate(sources)
            for b in range(count)
        )

    return pl.pallas_call(
        kernel,
        in_specs=[pl.BlockSpec(memory_space=pltpu.VMEM)] * len(children),
        out_specs=pl.BlockSpec(memory_space=pl.ANY),
        out_shape=jax.ShapeDtypeStruct((count, len(children), rows, piece), children[0].dtype),
        scratch_shapes=[pltpu.SemaphoreType.DMA((len(children), count))],
        cost_estimate=pl.CostEstimate(flops=0, transcendentals=0, bytes_accessed=8 * rows * width),
        compiler_params=pltpu.CompilerParams(vmem_limit_bytes=VMEM_BYTES),
        name="split_columns",
    )(*children)


def gather_blocks(table, blocks, groups, size):
    _, height, piece = blocks.shape

    def kernel(table_ref, source, *refs):
        outs, sems = refs[:-1], refs[-1]
        copy_all(
            [
                pltpu.make_async_copy(
                    source.at[table_ref[g * size + n]], outs[g].at[n], sems.at[g * size + n]
                )
                for g in range(groups)
                for n in range(size)
            ]
        )

    anyspec = pl.BlockSpec(memory_space=pl.ANY)
    return pl.pallas_call(
        kernel,
        grid_spec=pltpu.PrefetchScalarGridSpec(
            num_scalar_prefetch=1,
            grid=(1,),
            in_specs=[pl.BlockSpec(blocks.shape, lambda i, t: (0, 0, 0))],
            out_specs=[anyspec] * groups,
            scratch_shapes=[pltpu.SemaphoreType.DMA((groups * size,))],
        ),
        out_shape=[jax.ShapeDtypeStruct((size, height, piece), blocks.dtype)] * groups,
        cost_estimate=pl.CostEstimate(flops=0, transcendentals=0, bytes_accessed=4 * groups * size * height * piece),
        compiler_params=pltpu.CompilerParams(vmem_limit_bytes=VMEM_BYTES),
        name="gather_blocks",
    )(table, blocks)


def routing_tables(maps, rank, row_count, local_blocks, per_source, base, extra):
    children = len(maps)
    blocks = maps[0].shape[0]
    sent_base = row_count * children * base
    sent_extra = children * row_count * extra
    lists = [children * base]
    shapes = [(max(sent_base, 1),), (max(sent_extra, 1),)]
    for size in lists:
        shapes += [(size,)] * 3
    shapes += [(1,)] + [(local_blocks,)] * (2 * children)

    def kernel(rank_ref, *refs):
        map_refs = refs[:children]
        base_ref, extra_ref = refs[children : children + 2]
        outs = refs[children + 2 : children + 2 + 3 * len(lists)]
        state_ref, *by_row = refs[children + 2 + 3 * len(lists) : -2]
        counts, where = refs[-2:]
        mine = rank_ref[0]

        def clear(ref, size, value):
            def body(i, _):
                ref[i] = jnp.int32(value)
                return 0

            lax.fori_loop(0, size, body, 0)

        clear(base_ref, shapes[0][0], 0)
        clear(extra_ref, shapes[1][0], 0)
        clear(counts, children * row_count, 0)
        clear(where, children * local_blocks, -1)
        for c in range(children):

            def body(i, _, c=c):
                value = map_refs[c][i]
                owner = value // local_blocks
                far = lax.rem(owner + row_count - mine, row_count)
                at = counts[c * row_count + owner]
                counts[c * row_count + owner] = at + 1
                block = (i // per_source) * (children * per_source) + c * per_source + lax.rem(i, per_source)

                @pl.when(at < base)
                def _():
                    base_ref[(far * children + c) * base + at] = block

                if extra:

                    @pl.when(at >= base)
                    def _():
                        extra_ref[(c * row_count + far) * extra + at - base] = block

                @pl.when(owner == mine)
                def _():
                    where[c * local_blocks + value - owner * local_blocks] = at

                return 0

            lax.fori_loop(0, blocks, body, 0)

        def listed(out, size, chosen):
            rows_ref, valid_ref, slot_ref = out

            def put(at, row, slot):
                rows_ref[at] = row
                valid_ref[at] = jnp.int32(1)
                slot_ref[at] = slot
                return at + 1

            def body(t, at):
                for c, low, high, shift in chosen:
                    slot = where[c * local_blocks + t]
                    hit = (slot >= low) & (slot < high)

                    @pl.when(hit)
                    def _(at=at, slot=slot, low=low, shift=shift):
                        put(at, t, slot - low + shift)

                    at = at + hit.astype(jnp.int32)
                return at

            filled = lax.fori_loop(0, local_blocks, body, jnp.int32(0))
            last = jnp.maximum(filled - 1, 0)
            row = jnp.where(filled > 0, rows_ref[last], 0)
            slot = jnp.where(filled > 0, slot_ref[last], 0)

            def pad(i, _):
                @pl.when(i >= filled)
                def _():
                    rows_ref[i] = row
                    valid_ref[i] = jnp.int32(0)
                    slot_ref[i] = slot

                return 0

            lax.fori_loop(0, size, pad, 0)

        clear(outs[0], lists[0], 0)
        clear(outs[2], lists[0], 0)
        listed(outs, lists[0], [(c, 0, base, c * base) for c in range(children)])
        for c in range(children):

            def find(t, before, c=c):
                slot = where[c * local_blocks + t] - base
                hit = (slot >= 0) & (slot < extra)
                before = jnp.where(hit, slot, before)
                by_row[2 * c][t] = before
                by_row[2 * c + 1][t] = hit.astype(jnp.int32)
                return before

            lax.fori_loop(0, local_blocks, find, jnp.int32(0))

        state = jnp.int32(0)
        for c in range(children):
            busy = jnp.int32(0)
            over = jnp.int32(0)
            for k in range(row_count):
                more = counts[c * row_count + k] > base
                busy = jnp.where(more, k, busy)
                over = over + more.astype(jnp.int32)
            state = state * (row_count + 1) + jnp.where(over > 1, row_count, busy)
        state_ref[0] = state

    smem = pl.BlockSpec(memory_space=pltpu.SMEM)
    return pl.pallas_call(
        kernel,
        in_specs=[smem] * (1 + children),
        out_specs=[smem] * len(shapes),
        out_shape=[jax.ShapeDtypeStruct(shape, jnp.int32) for shape in shapes],
        scratch_shapes=[
            pltpu.SMEM((children * row_count,), jnp.int32),
            pltpu.SMEM((children * local_blocks,), jnp.int32),
        ],
        name="routing_tables",
    )(rank, *maps)


def down_the_rows(own, root, row_rank, row_count):
    kept = [jnp.where(row_rank == root, own, 0)]
    for step in (1, -1):
        moving, k, hop = own, root, 1
        while 0 <= k + step < row_count:
            moving = lax.ppermute(moving, "row", [(k, k + step)])
            kept.append(moving)
            k += step
            hop += 1
    return kept


def around(value, far, row_count):
    return lax.ppermute(value, "row", [(k, (k + far) % row_count) for k in range(row_count)])


def extra_exchange(state, groups, row_count):
    def branch(code):
        choices = []
        for _ in groups:
            choices.append(code % (row_count + 1))
            code //= row_count + 1
        choices = choices[::-1]

        def run(*flat):
            got = []
            for c, owner in enumerate(choices):
                for far in range(1, row_count):
                    value = flat[c * (row_count - 1) + far - 1]
                    if owner == row_count:
                        got.append(around(value, far, row_count))
                    else:
                        got.append(lax.ppermute(value, "row", [((owner - far) % row_count, owner)]))
            return tuple(got)

        return run

    flat = [value for group in groups for value in group[1:]]
    branches = [branch(code) for code in range((row_count + 1) ** len(groups))]
    got = lax.switch(state, branches, *flat)
    step = row_count - 1
    return [[group[0], *got[c * step : (c + 1) * step]] for c, group in enumerate(groups)]


def per_device(front_panel, front_slab, child_one, child_two, map_one, map_two):
    rows_dev, slab_width = front_slab.shape
    panel_width = front_panel.shape[1]
    child_blocks = map_one.shape[0]
    row_count = lax.axis_size("row")
    col_count = lax.axis_size("col")
    row_rank = lax.axis_index("row").astype(jnp.int32)
    col_rank = lax.axis_index("col").astype(jnp.int32)
    local_blocks = rows_dev // BLK
    capacity = 2 * child_blocks // row_count
    base = capacity // 2 if row_count <= 4 else capacity
    extra = capacity - base
    head = 2 * P_SIZE
    panel = front_panel.T
    piece = slab_width // row_count

    def spread(value):
        return [value] + [
            lax.ppermute(value, "col", [(k, k ^ far) for k in range(col_count)]) for far in range(1, col_count)
        ]

    pieces = split_columns((child_one, child_two), col_count)
    panel, pieces = lax.optimization_barrier((panel, pieces))
    got = lax.all_to_all(pieces, "col", split_axis=0, concat_axis=0, tiled=True)
    got = got.reshape(2 * child_blocks, BLK, piece)
    panel_later, got = lax.optimization_barrier((panel, got))

    top = sum(
        (lax.ppermute(panel[:, :head], "row", [(0, k)]) for k in range(1, row_count)),
        jnp.where(row_rank == 0, panel[:, :head], 0),
    )
    even = col_count & (col_count - 1) == 0
    part_rank = col_rank.reshape(1) if even else jnp.zeros((1,), jnp.int32)
    top_parts = spread(top) if even else [lax.all_gather(top, "col", axis=0, tiled=True)]

    segments = []
    wanted_stop = head + col_count * slab_width
    for root in range(row_count):
        low = max(head, root * rows_dev) - root * rows_dev
        high = min(wanted_stop, (root + 1) * rows_dev) - root * rows_dev
        if high > low:
            segments.append(down_the_rows(panel[:, low:high], root, row_rank, row_count))

    rank = row_rank.reshape(1)
    tables = routing_tables(
        (map_one, map_two), rank, row_count, local_blocks, child_one.shape[0] // BLK, base, extra
    )
    base_table, extra_table = tables[:2]
    base_lists, state, where = tables[2:5], tables[5][0], tables[6:10]
    groups = []
    if extra:
        groups = gather_blocks(extra_table, got, 2 * row_count, extra)
        groups = extra_exchange(state, [groups[:row_count], groups[row_count:]], row_count)
        got, groups, segments = lax.optimization_barrier((got, groups, segments))
    wanted = jnp.concatenate([sum(kept[1:], kept[0]) for kept in segments], 1)
    sent = gather_blocks(base_table, got, row_count, 2 * base)
    arrived = [sent[0]]
    for far in range(1, row_count):
        arrived.append(around(sent[far], far, row_count))

    parts = 2 if rows_dev % (2 * 512) == 0 else 1
    part = rows_dev // parts
    gathered = [
        lax.all_gather(panel_later[:, n * part : (n + 1) * part], "col", axis=0, tiled=True)
        for n in range(parts)
    ]
    wanted = lax.all_to_all(wanted, "col", split_axis=1, concat_axis=0, tiled=True)

    half = factor_first(part_rank, top_parts)
    inv_high, inv_low = factor_second(half)
    b_high, b_low = slab_rows(jnp.zeros((1,), jnp.int32), inv_high, inv_low, [wanted])
    skipped = jnp.clip(head // BLK - row_rank * local_blocks, 0, local_blocks).reshape(1)
    owns, slab = [], None
    for n in range(parts):
        f_high, f_low, own = panel_rows(inv_high, inv_low, gathered[n], col_rank.reshape(1), panel_width)
        owns.append(own)
        slab = update_slab(
            rank, skipped, where if extra else [], f_high, f_low, b_high, b_low, front_slab, groups, slab, n * part // BLK
        )
    own = jnp.concatenate(owns, 1)
    slab = place_blocks(rank, base_lists, arrived, slab)
    return (own.T, slab)


def solution(mesh):
    in_specs = (P("row", "col"), P("row", "col"), P("col", "row"), P("col", "row"), P(), P())
    out_specs = (P("row", "col"), P("row", "col"))
    return jax.shard_map(per_device, mesh=mesh, in_specs=in_specs, out_specs=out_specs, check_vma=False)
```

```python
import functools

import jax
import jax.numpy as jnp
from jax import lax
from jax.experimental import pallas as pl
from jax.experimental.pallas import tpu as pltpu
from jax.sharding import PartitionSpec as P


P_SIZE = 256
BLK = 256
SUB = 32
GROUP = 4
VMEM_BYTES = 56 * 1024 * 1024


def split_pair(value):
    high = value.astype(jnp.bfloat16)
    low = (value - high.astype(jnp.float32)).astype(jnp.bfloat16)
    return high, low


def dot3(a_high, a_low, b_high, b_low):
    def one(x, y):
        return jnp.dot(x, y, preferred_element_type=jnp.float32)

    return one(a_high, b_high) + (one(a_low, b_high) + one(a_high, b_low))


def exact_dot(a, b, contract):
    return lax.dot_general(
        a,
        b,
        (contract, ((), ())),
        precision=lax.Precision.HIGHEST,
        preferred_element_type=jnp.float32,
    )


def block_inverse(block):
    rows = lax.broadcasted_iota(jnp.int32, (SUB, SUB), 0)
    cols = lax.broadcasted_iota(jnp.int32, (SUB, SUB), 1)
    unit = (rows == cols).astype(jnp.float32)
    both = jnp.concatenate([block, unit, jnp.zeros((SUB, 128 - 2 * SUB), jnp.float32)], 1)
    row_of = lax.broadcasted_iota(jnp.int32, (SUB, 128), 0)
    scale = jnp.zeros((SUB, 128), jnp.float32)
    for j in range(0, SUB, GROUP):
        spread = [jnp.broadcast_to(both[:, j + k : j + k + 1], (SUB, 128)) for k in range(GROUP)]
        for k in range(GROUP):
            row = j + k
            pivot = jnp.broadcast_to(spread[k][row : row + 1, :], (SUB, 128))
            scale = jnp.where(row_of == row, pivot, scale)
            factor = jnp.where(row_of > row, spread[k] * (1.0 / pivot), 0.0)
            for m in range(k + 1, GROUP):
                spread[m] = spread[m] - factor * spread[m][row : row + 1, :]
            both = both - factor * both[row : row + 1, :]
    return (both / jnp.sqrt(scale))[:, SUB : 2 * SUB]


def inverse_steps(work_ref, first, last):
    size = work_ref.shape[0]
    for start in range(first, last, SUB):
        stop = start + SUB
        inverse = block_inverse(work_ref[start:stop, start:stop])
        lanes = lax.broadcasted_iota(jnp.int32, (SUB, size), 1)
        inside = (lanes >= start) & (lanes < stop)
        rows = exact_dot(inverse, jnp.where(inside, 0.0, work_ref[start:stop, :]), ((1,), (0,)))
        wide = jnp.concatenate([inverse] * (128 // SUB), 1)
        wide = jnp.concatenate([wide] * (size // 128), 1)
        rows = jnp.where(inside, wide, rows)
        if stop < size:
            below = exact_dot(work_ref[stop:size, start:stop], inverse, ((1,), (1,)))
            lanes_b = lax.broadcasted_iota(jnp.int32, (size - stop, size), 1)
            inside_b = (lanes_b >= start) & (lanes_b < stop)
            kept = jnp.where(inside_b, 0.0, work_ref[stop:size, :])
            work_ref[stop:size, :] = kept - exact_dot(below, rows, ((1,), (0,)))
        work_ref[start:stop, :] = jnp.where(lanes < stop, rows, 0.0)


def first_half_kernel(rank_ref, *refs):
    parts, work_ref = refs[:-1], refs[-1]
    height = parts[0].shape[0]
    for far, part in enumerate(parts):
        start = jnp.bitwise_xor(rank_ref[0], far) * height
        work_ref[pl.ds(pl.multiple_of(start, 8), height), :] = part[...]
    inverse_steps(work_ref, 0, P_SIZE)


def second_half_kernel(half_ref, high_ref, low_ref, work_ref):
    work_ref[...] = half_ref[...]
    inverse_steps(work_ref, P_SIZE, half_ref.shape[0])
    high, low = split_pair(work_ref[...])
    high_ref[...] = high
    low_ref[...] = low


def factor_first(rank, parts):
    size = parts[0].shape[1]
    return pl.pallas_call(
        first_half_kernel,
        in_specs=[pl.BlockSpec(memory_space=pltpu.SMEM)] + [pl.BlockSpec(memory_space=pltpu.VMEM)] * len(parts),
        out_shape=jax.ShapeDtypeStruct((size, size), jnp.float32),
        compiler_params=pltpu.CompilerParams(vmem_limit_bytes=VMEM_BYTES),
        cost_estimate=pl.CostEstimate(flops=size * size * 60000, transcendentals=0, bytes_accessed=2 * size * size * 4),
        name="factor_first",
    )(rank, *parts)


def factor_second(half):
    size = half.shape[0]
    pair = jax.ShapeDtypeStruct((size, size), jnp.bfloat16)
    return pl.pallas_call(
        second_half_kernel,
        out_shape=(pair, pair),
        scratch_shapes=[pltpu.VMEM((size, size), jnp.float32)],
        compiler_params=pltpu.CompilerParams(vmem_limit_bytes=VMEM_BYTES),
        cost_estimate=pl.CostEstimate(flops=size * size * 60000, transcendentals=0, bytes_accessed=2 * size * size * 4),
        name="factor_second",
    )(half)


def panel_kernel(rank_ref, high_ref, low_ref, panel_ref, fhigh_ref, flow_ref, own_ref, work_ref):
    p_high, p_low = split_pair(panel_ref[...])
    work_ref[...] = dot3(high_ref[...], low_ref[...], p_high, p_low)
    own = own_ref.shape[0]
    own_ref[...] = work_ref[pl.ds(pl.multiple_of(rank_ref[0] * own, 8), own), :]
    f_high, f_low = split_pair(work_ref[...].T)
    fhigh_ref[...] = f_high
    flow_ref[...] = f_low


def panel_rows(high, low, gathered, rank, own):
    size, rows = gathered.shape
    tile = 512
    pair = jax.ShapeDtypeStruct((rows, size), jnp.bfloat16)
    return pl.pallas_call(
        panel_kernel,
        grid_spec=pltpu.PrefetchScalarGridSpec(
            num_scalar_prefetch=1,
            grid=(rows // tile,),
            in_specs=[
                pl.BlockSpec((size, size), lambda i, r: (0, 0)),
                pl.BlockSpec((size, size), lambda i, r: (0, 0)),
                pl.BlockSpec((size, tile), lambda i, r: (0, i)),
            ],
            out_specs=[
                pl.BlockSpec((tile, size), lambda i, r: (i, 0)),
                pl.BlockSpec((tile, size), lambda i, r: (i, 0)),
                pl.BlockSpec((own, tile), lambda i, r: (0, i)),
            ],
            scratch_shapes=[pltpu.VMEM((size, tile), jnp.float32)],
        ),
        out_shape=(pair, pair, jax.ShapeDtypeStruct((own, rows), jnp.float32)),
        compiler_params=pltpu.CompilerParams(vmem_limit_bytes=VMEM_BYTES),
        cost_estimate=pl.CostEstimate(flops=6 * rows * size * size, transcendentals=0, bytes_accessed=8 * rows * size),
        name="panel_rows",
    )(rank, high, low, gathered)


def slab_rows_kernel(rank_ref, high_ref, low_ref, *refs):
    parts = refs[:-3]
    bhigh_ref, blow_ref, work_ref = refs[-3:]
    height = parts[0].shape[0]
    for far, part in enumerate(parts):
        start = jnp.bitwise_xor(rank_ref[0], far) * height
        work_ref[pl.ds(pl.multiple_of(start, 8), height), :] = part[...]
    p_high, p_low = split_pair(work_ref[...])
    b_high, b_low = split_pair(dot3(high_ref[...], low_ref[...], p_high, p_low))
    bhigh_ref[...] = b_high
    blow_ref[...] = b_low


def slab_rows(rank, high, low, parts):
    size = high.shape[0]
    height, rows = parts[0].shape
    tile = 512
    pair = jax.ShapeDtypeStruct((size, rows), jnp.bfloat16)
    whole = pl.BlockSpec((size, size), lambda i, r: (0, 0))
    out = pl.BlockSpec((size, tile), lambda i, r: (0, i))
    return pl.pallas_call(
        slab_rows_kernel,
        grid_spec=pltpu.PrefetchScalarGridSpec(
            num_scalar_prefetch=1,
            grid=(rows // tile,),
            in_specs=[whole, whole] + [pl.BlockSpec((height, tile), lambda i, r: (0, i))] * len(parts),
            out_specs=[out, out],
            scratch_shapes=[pltpu.VMEM((size, tile), jnp.float32)],
        ),
        out_shape=(pair, pair),
        compiler_params=pltpu.CompilerParams(vmem_limit_bytes=VMEM_BYTES),
        cost_estimate=pl.CostEstimate(flops=6 * rows * size * size, transcendentals=0, bytes_accessed=8 * rows * size),
        name="slab_rows",
    )(rank, high, low, *parts)


def add_stacked(block, out_ref):
    count, _, _, piece = block.shape
    for a in range(count):
        cols = slice(a * piece, (a + 1) * piece)
        out_ref[:, cols] = out_ref[:, cols] + block[a, 0].astype(jnp.float32)


def add_around(rank, pieces, out_ref):
    count = len(pieces)
    piece = pieces[0].shape[2]

    def add(part, cols):
        out_ref[:, cols] = out_ref[:, cols] + part[0].astype(jnp.float32)

    for far in range(count):
        source = lax.rem(rank + count - far, count)
        if piece % 128 == 0:
            add(pieces[far], pl.ds(pl.multiple_of(source * piece, 128), piece))
        else:
            for a in range(count):
                pl.when(source == a)(functools.partial(add, pieces[far], slice(a * piece, (a + 1) * piece)))


def update_kernel(first, groups, rank_ref, skip_ref, *refs):
    where, refs = refs[: 2 * groups], refs[2 * groups :]
    fhigh_ref, flow_ref, bhigh_ref, blow_ref, slab_ref = refs[:5]
    out_ref = refs[-1]
    step = pl.program_id(0) + first

    @pl.when(step < skip_ref[0])
    def _():
        out_ref[...] = slab_ref[...]

    @pl.when(step >= skip_ref[0])
    def _():
        out_ref[...] = slab_ref[...] - dot3(fhigh_ref[...], flow_ref[...], bhigh_ref[...], blow_ref[...])

    for c in range(groups):
        count = (len(refs) - 6) // groups
        pieces = refs[5 + c * count : 5 + (c + 1) * count]

        @pl.when(where[2 * c + 1][step] > 0)
        def _(pieces=pieces):
            add_around(rank_ref[0], pieces, out_ref)


def update_slab(rank, skipped, where, f_high, f_low, b_high, b_low, slab, groups, done, first):
    rows, width = slab.shape
    part, size = f_high.shape
    rowspec = pl.BlockSpec((BLK, size), lambda i, *t: (i, 0))
    bspec = pl.BlockSpec((size, width), lambda i, *t: (0, 0))
    tile = pl.BlockSpec((BLK, width), lambda i, *t: (i + first, 0))
    pieces, specs = [], []
    for c, group in enumerate(groups):
        piece = group[0].shape[2]
        pieces += group
        specs += [pl.BlockSpec((1, BLK, piece), lambda i, *t, c=c: (t[2 + 2 * c][i + first], 0, 0))] * len(group)
    before = [] if done is None else [done]
    kernel = functools.partial(update_kernel, first, len(groups))
    if before:
        inner = kernel

        def kernel(*refs):
            inner(*refs[:-2], refs[-1])

    return pl.pallas_call(
        kernel,
        grid_spec=pltpu.PrefetchScalarGridSpec(
            num_scalar_prefetch=2 + 2 * len(groups),
            grid=(part // BLK,),
            in_specs=[rowspec, rowspec, bspec, bspec, tile]
            + specs
            + [pl.BlockSpec(memory_space=pl.ANY)] * len(before),
            out_specs=tile,
        ),
        out_shape=jax.ShapeDtypeStruct((rows, width), jnp.float32),
        input_output_aliases={2 + 2 * len(groups) + 5 + len(pieces): 0} if before else {},
        compiler_params=pltpu.CompilerParams(vmem_limit_bytes=VMEM_BYTES),
        cost_estimate=pl.CostEstimate(flops=6 * part * size * width, transcendentals=0, bytes_accessed=8 * part * width),
        name="update_slab",
    )(rank, skipped, *where, f_high, f_low, b_high, b_low, slab, *pieces, *before)


def place_kernel(rank_ref, rows_ref, valid_ref, slot_ref, *refs):
    pieces = refs[:-2]
    slab_ref, out_ref = refs[-2:]
    step = pl.program_id(0)
    first = (step == 0) | (rows_ref[step] != rows_ref[jnp.maximum(step - 1, 0)])

    @pl.when(first)
    def _():
        out_ref[...] = slab_ref[...]

    @pl.when(valid_ref[step] > 0)
    def _():
        if len(pieces) == 1:
            add_stacked(pieces[0], out_ref)
        else:
            add_around(rank_ref[0], pieces, out_ref)


def place_blocks(rank, lists, pieces, slab):
    rows, width = slab.shape
    tile = pl.BlockSpec((BLK, width), lambda i, k, t, v, s: (t[i], 0))
    if len(pieces) == 1:
        count, slots, _, piece = pieces[0].shape
        part = pl.BlockSpec((count, 1, BLK, piece), lambda i, k, t, v, s: (0, s[i], 0, 0))
    else:
        slots, _, piece = pieces[0].shape
        part = pl.BlockSpec((1, BLK, piece), lambda i, k, t, v, s: (s[i], 0, 0))
    return pl.pallas_call(
        place_kernel,
        grid_spec=pltpu.PrefetchScalarGridSpec(
            num_scalar_prefetch=4,
            grid=(slots,),
            in_specs=[part] * len(pieces) + [tile],
            out_specs=tile,
        ),
        out_shape=jax.ShapeDtypeStruct((rows, width), jnp.float32),
        input_output_aliases={4 + len(pieces): 0},
        compiler_params=pltpu.CompilerParams(vmem_limit_bytes=VMEM_BYTES),
        cost_estimate=pl.CostEstimate(flops=0, transcendentals=0, bytes_accessed=8 * slots * BLK * width),
        name="place_blocks",
    )(rank, *lists, *pieces, slab)


def copy_all(copies):
    copies = list(copies)
    for copy in copies:
        copy.start()
    for copy in copies:
        copy.wait()


def split_columns(children, count):
    rows, width = children[0].shape
    piece = width // count
    if piece % 128:
        return jnp.stack([child.reshape(rows, count, piece).transpose(1, 0, 2) for child in children], 1)

    def kernel(*refs):
        sources, out, sems = refs[:-2], refs[-2], refs[-1]
        copy_all(
            pltpu.make_async_copy(source.at[:, b * piece : (b + 1) * piece], out.at[b, n], sems.at[n, b])
            for n, source in enumerate(sources)
            for b in range(count)
        )

    return pl.pallas_call(
        kernel,
        in_specs=[pl.BlockSpec(memory_space=pltpu.VMEM)] * len(children),
        out_specs=pl.BlockSpec(memory_space=pl.ANY),
        out_shape=jax.ShapeDtypeStruct((count, len(children), rows, piece), children[0].dtype),
        scratch_shapes=[pltpu.SemaphoreType.DMA((len(children), count))],
        cost_estimate=pl.CostEstimate(flops=0, transcendentals=0, bytes_accessed=8 * rows * width),
        compiler_params=pltpu.CompilerParams(vmem_limit_bytes=VMEM_BYTES),
        name="split_columns",
    )(*children)


def gather_blocks(table, blocks, groups, size):
    _, height, piece = blocks.shape

    def kernel(table_ref, source, *refs):
        outs, sems = refs[:-1], refs[-1]

        def copies(n):
            return [
                pltpu.make_async_copy(source.at[table_ref[g * size + n]], outs[g].at[n], sems.at[g * size + n])
                for g in range(groups)
            ]

        def start(n, _):
            for copy in copies(n):
                copy.start()
            return 0

        def wait(n, _):
            for copy in copies(n):
                copy.wait()
            return 0

        lax.fori_loop(0, size, start, 0)
        lax.fori_loop(0, size, wait, 0)

    anyspec = pl.BlockSpec(memory_space=pl.ANY)
    return pl.pallas_call(
        kernel,
        grid_spec=pltpu.PrefetchScalarGridSpec(
            num_scalar_prefetch=1,
            grid=(1,),
            in_specs=[pl.BlockSpec(blocks.shape, lambda i, t: (0, 0, 0))],
            out_specs=[anyspec] * groups,
            scratch_shapes=[pltpu.SemaphoreType.DMA((groups * size,))],
        ),
        out_shape=[jax.ShapeDtypeStruct((size, height, piece), blocks.dtype)] * groups,
        cost_estimate=pl.CostEstimate(flops=0, transcendentals=0, bytes_accessed=4 * groups * size * height * piece),
        compiler_params=pltpu.CompilerParams(vmem_limit_bytes=VMEM_BYTES),
        name="gather_blocks",
    )(table, blocks)


def routing_tables(maps, rank, row_count, local_blocks, per_source, base, extra):
    children = len(maps)
    blocks = maps[0].shape[0]
    sent_base = row_count * children * base
    sent_extra = children * row_count * extra
    lists = [children * base]
    shapes = [(max(sent_base, 1),), (max(sent_extra, 1),)]
    for size in lists:
        shapes += [(size,)] * 3
    shapes += [(children,)] + [(local_blocks,)] * (2 * children)

    def kernel(rank_ref, *refs):
        map_refs = refs[:children]
        base_ref, extra_ref = refs[children : children + 2]
        outs = refs[children + 2 : children + 2 + 3 * len(lists)]
        state_ref, *by_row = refs[children + 2 + 3 * len(lists) : -2]
        counts, where = refs[-2:]
        mine = rank_ref[0]

        def clear(ref, size, value):
            def body(i, _):
                ref[i] = jnp.int32(value)
                return 0

            lax.fori_loop(0, size, body, 0)

        clear(base_ref, shapes[0][0], 0)
        clear(extra_ref, shapes[1][0], 0)
        clear(counts, children * row_count, 0)
        clear(where, children * local_blocks, -1)
        for c in range(children):

            def body(i, _, c=c):
                value = map_refs[c][i]
                owner = value // local_blocks
                far = lax.rem(owner + row_count - mine, row_count)
                at = counts[c * row_count + owner]
                counts[c * row_count + owner] = at + 1
                block = (i // per_source) * (children * per_source) + c * per_source + lax.rem(i, per_source)

                @pl.when(at < base)
                def _():
                    base_ref[(far * children + c) * base + at] = block

                if extra:

                    @pl.when(at >= base)
                    def _():
                        extra_ref[(c * row_count + far) * extra + at - base] = block

                @pl.when(owner == mine)
                def _():
                    where[c * local_blocks + value - owner * local_blocks] = at

                return 0

            lax.fori_loop(0, blocks, body, 0)

        def listed(out, size, chosen):
            rows_ref, valid_ref, slot_ref = out

            def put(at, row, slot):
                rows_ref[at] = row
                valid_ref[at] = jnp.int32(1)
                slot_ref[at] = slot
                return at + 1

            def body(t, at):
                for c, low, high, shift in chosen:
                    slot = where[c * local_blocks + t]
                    hit = (slot >= low) & (slot < high)

                    @pl.when(hit)
                    def _(at=at, slot=slot, low=low, shift=shift):
                        put(at, t, slot - low + shift)

                    at = at + hit.astype(jnp.int32)
                return at

            filled = lax.fori_loop(0, local_blocks, body, jnp.int32(0))
            last = jnp.maximum(filled - 1, 0)
            row = jnp.where(filled > 0, rows_ref[last], 0)
            slot = jnp.where(filled > 0, slot_ref[last], 0)

            def pad(i, _):
                @pl.when(i >= filled)
                def _():
                    rows_ref[i] = row
                    valid_ref[i] = jnp.int32(0)
                    slot_ref[i] = slot

                return 0

            lax.fori_loop(0, size, pad, 0)

        clear(outs[0], lists[0], 0)
        clear(outs[2], lists[0], 0)
        listed(outs, lists[0], [(c, 0, base, c * base) for c in range(children)])
        for c in range(children):

            def find(t, before, c=c):
                slot = where[c * local_blocks + t] - base
                hit = (slot >= 0) & (slot < extra)
                before = jnp.where(hit, slot, before)
                by_row[2 * c][t] = before
                by_row[2 * c + 1][t] = hit.astype(jnp.int32)
                return before

            lax.fori_loop(0, local_blocks, find, jnp.int32(0))

        for c in range(children):
            busy = jnp.int32(0)
            over = jnp.int32(0)
            for k in range(row_count):
                more = counts[c * row_count + k] > base
                busy = jnp.where(more, k, busy)
                over = over + more.astype(jnp.int32)
            state_ref[c] = jnp.where(over > 1, row_count, busy)

    smem = pl.BlockSpec(memory_space=pltpu.SMEM)
    return pl.pallas_call(
        kernel,
        in_specs=[smem] * (1 + children),
        out_specs=[smem] * len(shapes),
        out_shape=[jax.ShapeDtypeStruct(shape, jnp.int32) for shape in shapes],
        scratch_shapes=[
            pltpu.SMEM((children * row_count,), jnp.int32),
            pltpu.SMEM((children * local_blocks,), jnp.int32),
        ],
        name="routing_tables",
    )(rank, *maps)


def down_the_rows(own, root, row_rank, row_count):
    kept = [jnp.where(row_rank == root, own, 0)]
    for step in (1, -1):
        moving, k, hop = own, root, 1
        while 0 <= k + step < row_count:
            moving = lax.ppermute(moving, "row", [(k, k + step)])
            kept.append(moving)
            k += step
            hop += 1
    return kept


def around(value, far, row_count):
    return lax.ppermute(value, "row", [(k, (k + far) % row_count) for k in range(row_count)])


def extra_exchange(state, group, row_count, work, *values):
    def branch(owner):
        def run(group, values):
            got = []
            for far in range(1, row_count):
                if owner == row_count:
                    got.append(around(group[far], far, row_count))
                else:
                    got.append(lax.ppermute(group[far], "row", [((owner - far) % row_count, owner)]))
            return got, work(*values)

        return run

    got, done = lax.switch(state, [branch(owner) for owner in range(row_count + 1)], group, values)
    return [group[0], *got], done


def per_device(front_panel, front_slab, child_one, child_two, map_one, map_two):
    rows_dev, slab_width = front_slab.shape
    panel_width = front_panel.shape[1]
    child_blocks = map_one.shape[0]
    row_count = lax.axis_size("row")
    col_count = lax.axis_size("col")
    row_rank = lax.axis_index("row").astype(jnp.int32)
    col_rank = lax.axis_index("col").astype(jnp.int32)
    local_blocks = rows_dev // BLK
    capacity = 2 * child_blocks // row_count
    base = capacity // 2 if row_count <= 4 else capacity
    extra = capacity - base
    head = 2 * P_SIZE
    panel = front_panel.T
    piece = slab_width // row_count

    def spread(value):
        return [value] + [
            lax.ppermute(value, "col", [(k, k ^ far) for k in range(col_count)]) for far in range(1, col_count)
        ]

    pieces = split_columns((child_one, child_two), col_count)
    panel, pieces = lax.optimization_barrier((panel, pieces))
    got = lax.all_to_all(pieces, "col", split_axis=0, concat_axis=0, tiled=True)
    got = got.reshape(2 * child_blocks, BLK, piece)
    panel_later, got = lax.optimization_barrier((panel, got))

    top = sum(
        (lax.ppermute(panel[:, :head], "row", [(0, k)]) for k in range(1, row_count)),
        jnp.where(row_rank == 0, panel[:, :head], 0),
    )
    even = col_count & (col_count - 1) == 0
    part_rank = col_rank.reshape(1) if even else jnp.zeros((1,), jnp.int32)
    top_parts = spread(top) if even else [lax.all_gather(top, "col", axis=0, tiled=True)]

    segments = []
    wanted_stop = head + col_count * slab_width
    for root in range(row_count):
        low = max(head, root * rows_dev) - root * rows_dev
        high = min(wanted_stop, (root + 1) * rows_dev) - root * rows_dev
        if high > low:
            segments.append(down_the_rows(panel[:, low:high], root, row_rank, row_count))

    rank = row_rank.reshape(1)
    tables = routing_tables(
        (map_one, map_two), rank, row_count, local_blocks, child_one.shape[0] // BLK, base, extra
    )
    base_table, extra_table = tables[:2]
    base_lists, states, where = tables[2:5], tables[5], tables[6:10]

    def base_gather(blocks):
        return gather_blocks(base_table, blocks, row_count, 2 * base)

    groups = []
    if extra:
        size = row_count * extra

        def extra_gather(blocks, c):
            return gather_blocks(extra_table[c * size : (c + 1) * size], blocks, row_count, extra)

        one = extra_gather(got, 0)
        one, two = extra_exchange(states[0], one, row_count, lambda blocks: extra_gather(blocks, 1), got)
        two, sent = extra_exchange(states[1], two, row_count, base_gather, got)
        groups, sent, segments = lax.optimization_barrier(([one, two], sent, segments))
    else:
        sent = base_gather(got)
    wanted = jnp.concatenate([sum(kept[1:], kept[0]) for kept in segments], 1)
    arrived = [sent[0]]
    for far in range(1, row_count):
        arrived.append(around(sent[far], far, row_count))

    parts = 2 if rows_dev % (2 * 512) == 0 else 1
    part = rows_dev // parts
    gathered = [
        lax.all_gather(panel_later[:, n * part : (n + 1) * part], "col", axis=0, tiled=True)
        for n in range(parts)
    ]
    wanted = lax.all_to_all(wanted, "col", split_axis=1, concat_axis=0, tiled=True)

    half = factor_first(part_rank, top_parts)
    inv_high, inv_low = factor_second(half)
    b_high, b_low = slab_rows(jnp.zeros((1,), jnp.int32), inv_high, inv_low, [wanted])
    skipped = jnp.clip(head // BLK - row_rank * local_blocks, 0, local_blocks).reshape(1)
    owns, slab = [], None
    for n in range(parts):
        f_high, f_low, own = panel_rows(inv_high, inv_low, gathered[n], col_rank.reshape(1), panel_width)
        owns.append(own)
        slab = update_slab(
            rank, skipped, where if extra else [], f_high, f_low, b_high, b_low, front_slab, groups, slab, n * part // BLK
        )
    own = jnp.concatenate(owns, 1)
    slab = place_blocks(rank, base_lists, arrived, slab)
    return (own.T, slab)


def solution(mesh):
    in_specs = (P("row", "col"), P("row", "col"), P("col", "row"), P("col", "row"), P(), P())
    out_specs = (P("row", "col"), P("row", "col"))
    return jax.shard_map(per_device, mesh=mesh, in_specs=in_specs, out_specs=out_specs, check_vma=False)
```
